512 devices in a mesh: depth: 8 (over y, core), tile: 16 (over z), brick: 4 (over x).
Axes of the slice: x: 4, y: 4, z: 16, core: 2. Of those that a mesh axis runs over, the one named last changes fastest.
Arguments:
- fragments: float32 [8, 64, 64, 2, 16, 128], P('depth', ('tile', 'brick')), may hold values from 0 to 0.61, as said below
- layer_rank: int32 [8, 64, 64, 2, 4, 128], P('depth', ('tile', 'brick')), may hold values from 0 to 3, as said below
- pixel_count: int32 [8, 64, 64, 2], P('depth', ('tile', 'brick')), may hold values from 1 to 128
- slot_count: int32 [8, 64, 64], P('depth', ('tile', 'brick')), may hold values from 0 to 2, as said below
- block_run: int32 [8, 64, 64, 2], P('depth', ('tile', 'brick')), may hold values from 0 to 255, as said below
- brick_order: int32 [8, 64], P('depth'), may hold values from 0 to 63, each once within a row
- interlace: int32 [256], replicated, may hold values from 0 to 255, as said below
Outputs:
- image: float32 [64, 8, 32, 4, 128], P(('tile', 'brick'), 'depth')
The draws below stay inside these ranges and needn't reach their ends.
Inputs may be any that keep to these rules, and one draw needn't show every extreme that they name: `fragments`: each entry is r, g, b, alpha with alpha at least 0.003 and each color between 0 and alpha. `layer_rank`: at every pixel the four ranks are 0, 1, 2 and 3 in some order. `slot_count`: in every slab some owner receives 2 live blocks from every brick. `block_run`: the slots that one brick sends to one owner name distinct strip slots. `brick_order`: each slab's ranks name every brick once. `interlace`: each value once; every aligned group of 32 consecutive entries holds exactly 4 values of each aligned range of 32 values.
All inputs are finite; a program needn't handle non-finite values.
Results may differ from the reference program's by a relative error of at most 0.0003.
Values sent between devices are 32-bit elements; how exact they have to be, the bound alone decides.
No kernel may reach another device: no remote copies, remote signals or barrier semaphores. Data moves between devices by JAX's collectives and lax.ppermute only.
A program may use at most 64 MiB of HBM per device.

```python
import math
import jax
import jax.numpy as jnp
from jax import lax

PIX = 128
CAP = 2
RUNS = 256
SLABS = 8
OWNERS = 64
Q = 32


def draw_fragments(key, part):
    alpha_key, color_key = jax.random.split(key)
    alpha_shape = (SLABS, OWNERS, OWNERS, CAP, 4, 1, PIX)
    color_shape = (SLABS, OWNERS, OWNERS, CAP, 4, 3, PIX)
    alpha = jnp.exp(jax.random.uniform(alpha_key, alpha_shape, jnp.float32, math.log(0.003), math.log(0.6)))
    color = alpha * jax.random.uniform(color_key, color_shape, jnp.float32)
    return jnp.concatenate([color, alpha], axis=5).reshape(SLABS, OWNERS, OWNERS, CAP, 16, PIX)


def draw_layer_rank(key, part):
    shape = (SLABS, OWNERS, OWNERS, CAP, 4, PIX)
    scores = jax.random.randint(key, shape, 0, 1 << 20) * 4 + lax.broadcasted_iota(jnp.int32, shape, 4)
    order = jnp.argsort(scores, axis=4)
    return jnp.argsort(order, axis=4).astype(jnp.int32)


def draw_slot_count(key, part):
    base_key, busy_key = jax.random.split(key)
    base = jax.random.randint(base_key, (SLABS, OWNERS, OWNERS), 0, CAP + 1)
    busy = jax.random.randint(busy_key, (SLABS,), 0, OWNERS)
    full = lax.broadcasted_iota(jnp.int32, (SLABS, OWNERS, OWNERS), 1) == busy[:, None, None]
    return jnp.where(full, CAP, base).astype(jnp.int32)


def draw_block_run(key, part):
    shape = (SLABS, OWNERS, OWNERS, RUNS)
    scores = jax.random.randint(key, shape, 0, 1 << 20) * RUNS + lax.broadcasted_iota(jnp.int32, shape, 3)
    return lax.top_k(scores, CAP)[1].astype(jnp.int32)


def draw_interlace(key, part):
    spread_key, shuffle_key = jax.random.split(key)
    per_tile = Q // SLABS
    tile_keys = jax.random.split(spread_key, SLABS)
    within = jax.vmap(lambda single: jax.random.permutation(single, Q))(tile_keys)
    base = lax.broadcasted_iota(jnp.int32, (SLABS, Q), 0) * Q
    screen = (within + base).reshape(SLABS, SLABS, per_tile)
    grouped = jnp.transpose(screen, (1, 0, 2)).reshape(SLABS, Q)
    piece_keys = jax.random.split(shuffle_key, SLABS)
    mixed = jax.vmap(lambda single, entries: jax.random.permutation(single, entries))(piece_keys, grouped)
    return mixed.reshape(RUNS).astype(jnp.int32)


def set_ends(drawn, rng, smallest, top_value):
    longest = drawn.shape.index(max(drawn.shape))
    spots = []
    for shift in (0, 1):
        where = [jax.random.randint(jax.random.fold_in(rng, axis), (), 0, length) for axis, length in enumerate(drawn.shape)]
        where[longest] = (where[longest] + shift) % drawn.shape[longest]
        spots.append(tuple(where))
    return drawn.at[spots[0]].set(smallest).at[spots[1]].set(top_value)


def setup_inputs(seed: int = 0) -> dict:
    keys = jax.random.split(jax.random.key(seed), 8)
    return {
        "fragments": draw_fragments(jax.random.fold_in(keys[7], 71), 0),
        "layer_rank": draw_layer_rank(jax.random.fold_in(keys[7], 71), 0),
        "pixel_count": set_ends(jax.random.randint(keys[2], (SLABS, OWNERS, OWNERS, CAP), 1, PIX + 1), jax.random.fold_in(keys[2], 1), 1, PIX).astype(jnp.int32),
        "slot_count": draw_slot_count(jax.random.fold_in(keys[7], 71), 0),
        "block_run": draw_block_run(jax.random.fold_in(keys[7], 71), 0),
        "brick_order": jax.vmap(lambda own: jax.random.permutation(own, OWNERS))(jax.random.split(keys[5], SLABS)).reshape((SLABS, OWNERS)).astype(jnp.int32),
        "interlace": draw_interlace(jax.random.fold_in(keys[7], 71), 0),
    }


def order_layers(layers, ranks, counts):
    width = layers.shape[-1]
    pixel = lax.broadcasted_iota(jnp.int32, counts.shape + (width,), 2)
    visible = (pixel < counts[:, :, None]).astype(jnp.float32)
    placed = []
    for position in range(4):
        chosen = jnp.zeros(layers.shape[:2] + layers.shape[3:], jnp.float32)
        for layer in range(4):
            picked = (ranks[:, :, layer, :] == position).astype(jnp.float32)
            chosen = chosen + picked[:, :, None, :] * layers[:, :, layer]
        placed.append(chosen * visible[:, :, None, :])
    return jnp.stack(placed, axis=2)


def blend(layers):
    result = layers[..., 3, :, :]
    for position in (2, 1, 0):
        front = layers[..., position, :, :]
        result = front + (1.0 - front[..., 3:4, :]) * result
    return result


def over(front, back):
    return front + (1.0 - front[..., 3:4, :]) * back


def compose_strip(blocks, live, runs, brick_rank, slots):
    keeping = jnp.log(1.0 - blocks[:, 3, :] * live[:, None])
    same = runs[:, None] == runs[None, :]
    before = brick_rank[None, :] < brick_rank[:, None]
    earlier = (same & before).astype(jnp.float32)
    passed = jnp.exp(jnp.dot(earlier, keeping, precision=lax.Precision.HIGHEST))
    shaded = (blocks * live[:, None, None] * passed[:, None, :]).reshape(blocks.shape[0], 4 * blocks.shape[-1])
    target = (lax.broadcasted_iota(jnp.int32, (slots, runs.shape[0]), 0) == runs[None, :]).astype(jnp.float32)
    strip = jnp.dot(target, shaded, precision=lax.Precision.HIGHEST)
    return strip.reshape(slots, 4, blocks.shape[-1])


def slab_image(pieces):
    fragments, layer_rank, pixel_count, slot_count, block_run, brick_order = pieces
    owners = fragments.shape[0]
    capacity = fragments.shape[2]
    width = fragments.shape[-1]
    layers = fragments.reshape(owners * owners, capacity, 4, 4, width)
    ordered = order_layers(layers, layer_rank.reshape(owners * owners, capacity, 4, width), pixel_count.reshape(owners * owners, capacity))
    blocks = blend(ordered).reshape(owners, owners, capacity, 4, width)

    def one_owner(target):
        incoming = lax.dynamic_index_in_dim(blocks, target, 1, keepdims=False).reshape(owners * capacity, 4, width)
        counts = lax.dynamic_index_in_dim(slot_count, target, 0, keepdims=False)
        runs = lax.dynamic_index_in_dim(block_run, target, 0, keepdims=False).reshape(owners * capacity)
        live = (lax.broadcasted_iota(jnp.int32, (owners, capacity), 1) < counts[:, None]).astype(jnp.float32).reshape(owners * capacity)
        brick_rank = jnp.repeat(brick_order, capacity)
        return compose_strip(incoming, live, runs, brick_rank, RUNS)

    return lax.map(one_owner, jnp.arange(owners, dtype=jnp.int32))


def reference(fragments, layer_rank, pixel_count, slot_count, block_run, brick_order, interlace):
    strips = lax.map(slab_image, (fragments, layer_rank, pixel_count, slot_count, block_run, brick_order))
    total = strips[0]
    for slab in range(1, SLABS):
        total = over(total, strips[slab])
    image = jnp.zeros_like(total).at[:, interlace].set(total)
    return image.reshape(OWNERS, SLABS, Q, 4, PIX)
```

```python
import jax
import jax.numpy as jnp
from jax import lax
from jax.experimental import pallas as pl
from jax.experimental.pallas import tpu as pltpu
from jax.sharding import PartitionSpec as P


def columns(row, first, rows, width):
    length = row.shape[1]
    place = lax.broadcasted_iota(jnp.int32, (rows, length), 1)
    own = lax.broadcasted_iota(jnp.int32, (rows, length), 0) + first
    spread = jnp.where(place == own, row.astype(jnp.float32), 0.0).astype(jnp.bfloat16)
    return jnp.dot(
        spread, jnp.ones((length, width), jnp.bfloat16), preferred_element_type=jnp.float32
    )


def halves(values):
    high = values.astype(jnp.bfloat16)
    low = (values - high.astype(jnp.float32)).astype(jnp.bfloat16)
    return high, low


def blend_kernel(capacity, fragments, ranks, counts, out):
    owners = out.shape[0] // (capacity * 4)
    width = out.shape[1]
    first = pl.program_id(0) * owners
    pixel = lax.broadcasted_iota(jnp.int32, (owners, width), 1).astype(jnp.float32)
    for slot in range(capacity):
        visible = pixel < columns(counts[slot : slot + 1, :], first, owners, width)
        rank = [ranks[pl.ds(slot * 4 + layer, owners, stride=capacity * 4), :] for layer in range(4)]
        entry = [
            [
                fragments[pl.ds(slot * 16 + layer * 4 + part, owners, stride=capacity * 16), :]
                for part in range(4)
            ]
            for layer in range(4)
        ]
        clear = [1.0 - entry[layer][3] for layer in range(4)]
        weight = [jnp.where(visible, 1.0, 0.0)] * 4
        for one in range(4):
            for two in range(one + 1, 4):
                ahead = rank[one] < rank[two]
                weight[two] = weight[two] * jnp.where(ahead, clear[one], 1.0)
                weight[one] = weight[one] * jnp.where(ahead, 1.0, clear[two])
        for part in range(4):
            mixed = entry[0][part] * weight[0]
            for layer in range(1, 4):
                mixed = mixed + entry[layer][part] * weight[layer]
            out[pl.ds(slot * 4 + part, owners, stride=capacity * 4), :] = mixed


def blend(fragments, ranks, counts, steps):
    owners, capacity, _, width = fragments.shape
    flat = fragments.reshape(owners * capacity * 16, width)
    flat_ranks = ranks.reshape(owners * capacity * 4, width)
    rows = owners * capacity // steps

    def kernel(*refs):
        blend_kernel(capacity, *refs)

    return pl.pallas_call(
        kernel,
        grid=(steps,),
        in_specs=[
            pl.BlockSpec((rows * 16, width), lambda i: (i, 0)),
            pl.BlockSpec((rows * 4, width), lambda i: (i, 0)),
            pl.BlockSpec((capacity, owners), lambda i: (0, 0)),
        ],
        out_specs=pl.BlockSpec((rows * 4, width), lambda i: (i, 0)),
        out_shape=jax.ShapeDtypeStruct((owners * capacity * 4, width), jnp.float32),
        name="blend",
    )(flat, flat_ranks, counts)


def plan_kernel(counts, runs, order, interlace, earlier, target):
    capacity, bricks = runs.shape
    slots = interlace.shape[1]
    total = capacity * bricks
    run = jnp.concatenate([runs[slot : slot + 1, :] for slot in range(capacity)], axis=1)
    rank = jnp.concatenate([order[...]] * capacity, axis=1)
    live = jnp.concatenate([jnp.where(counts[...] > slot, 1, 0) for slot in range(capacity)], axis=1) > 0
    run_of = columns(run, 0, total, total).astype(jnp.int32)
    rank_of = columns(rank, 0, total, total).astype(jnp.int32)
    ahead = (run_of == run) & (rank < rank_of) & live
    earlier[...] = jnp.where(ahead, 1.0, 0.0).astype(jnp.bfloat16)
    slot_id = lax.broadcasted_iota(jnp.int32, (slots, total), 0)
    landing = jnp.where(slot_id == run, 1.0, 0.0).astype(jnp.bfloat16)
    screen = jnp.dot(
        jnp.broadcast_to(interlace[...].astype(jnp.float32), (8, slots)).astype(jnp.bfloat16),
        landing,
        preferred_element_type=jnp.float32,
    )[0:1, :].astype(jnp.int32)
    target[...] = jnp.where((slot_id == screen) & live, 1.0, 0.0).astype(jnp.bfloat16)


def plan(counts, runs, order, interlace):
    capacity, bricks = runs.shape
    total = capacity * bricks
    slots = interlace.shape[1]
    return pl.pallas_call(
        plan_kernel,
        out_shape=(
            jax.ShapeDtypeStruct((total, total), jnp.bfloat16),
            jax.ShapeDtypeStruct((slots, total), jnp.bfloat16),
        ),
        name="plan",
    )(counts, runs, order, interlace)


def strip_kernel(capacity, blocks, earlier, target, out):
    bricks = blocks.shape[0] // (capacity * 4)
    tiles, _, share, width = out.shape

    def part_of(part):
        return jnp.concatenate(
            [blocks[pl.ds(slot * 4 + part, bricks, stride=capacity * 4), :] for slot in range(capacity)],
            axis=0,
        )

    def picked(matrix, values):
        high, low = halves(values)
        return jnp.dot(matrix, high, preferred_element_type=jnp.float32) + jnp.dot(
            matrix, low, preferred_element_type=jnp.float32
        )

    alpha = part_of(3)
    passed = jnp.exp(picked(earlier[...], jnp.log(1.0 - alpha)))
    shaded = jnp.concatenate([part_of(0) * passed, part_of(1) * passed, part_of(2) * passed, alpha * passed], axis=1)
    strip = picked(target[...], shaded)
    for tile in range(tiles):
        for part in range(4):
            out[tile, part] = strip[tile * share : (tile + 1) * share, part * width : (part + 1) * width]


def compose_strip(blocks, earlier, target, capacity, tiles):
    width = blocks.shape[1]
    slots = target.shape[0]

    def kernel(*refs):
        strip_kernel(capacity, *refs)

    return pl.pallas_call(
        kernel,
        out_shape=jax.ShapeDtypeStruct((tiles, 4, slots // tiles, width), jnp.float32),
        name="strip",
    )(blocks, earlier, target)


def stack_kernel(strips, out):
    slabs, _, share, _ = strips.shape
    total = [strips[slabs - 1, part] for part in range(4)]
    for slab in range(slabs - 2, -1, -1):
        clear = 1.0 - strips[slab, 3]
        total = [strips[slab, part] + clear * total[part] for part in range(4)]
    for part in range(4):
        out[pl.ds(part, share, stride=4), :] = total[part]


def stack(strips):
    _, _, share, width = strips.shape
    return pl.pallas_call(
        stack_kernel,
        out_shape=jax.ShapeDtypeStruct((share * 4, width), jnp.float32),
        name="stack",
    )(strips)


def shards(fragments, layer_rank, pixel_count, slot_count, block_run, brick_order, interlace):
    _, _, owners, capacity, _, width = fragments.shape
    slots = interlace.shape[0]
    tiles = lax.axis_size("depth")
    blocks = blend(
        fragments[0, 0],
        layer_rank[0, 0],
        pixel_count[0, 0].T,
        4,
    )
    sent = lax.all_to_all(
        blocks.reshape(owners, capacity * 4, width), ("tile", "brick"), split_axis=0, concat_axis=0, tiled=True
    )
    earlier, target = plan(slot_count[0], block_run[0, 0].T, brick_order, interlace.reshape(1, slots))
    strip = compose_strip(sent.reshape(owners * capacity * 4, width), earlier, target, capacity, tiles)
    strips = lax.all_to_all(strip, "depth", split_axis=0, concat_axis=0, tiled=True)
    return stack(strips).reshape(1, 1, slots // tiles, 4, width)


def solution(mesh):
    return jax.shard_map(
        shards,
        mesh=mesh,
        in_specs=(
            P("depth", ("tile", "brick"), None, None, None, None),
            P("depth", ("tile", "brick"), None, None, None),
            P("depth", ("tile", "brick"), None, None),
            P("depth", ("tile", "brick"), None),
            P("depth", ("tile", "brick"), None, None),
            P("depth", None),
            P(),
        ),
        out_specs=P(("tile", "brick"), "depth", None, None, None),
        check_vma=False,
    )
```

```python
import jax
import jax.numpy as jnp
import numpy as np
from jax import lax
from jax.experimental import pallas as pl
from jax.experimental.pallas import tpu as pltpu
from jax.sharding import PartitionSpec as P


def resident(array):
    return pltpu.with_memory_space_constraint(array, pltpu.VMEM)


def columns(row, rows, width):
    length = row.shape[1]
    place = lax.broadcasted_iota(jnp.int32, (rows, length), 1)
    own = lax.broadcasted_iota(jnp.int32, (rows, length), 0)
    spread = jnp.where(place == own, row.astype(jnp.float32), 0.0).astype(jnp.bfloat16)
    return jnp.dot(spread, jnp.ones((length, width), jnp.bfloat16), preferred_element_type=jnp.float32)


def reorder(row, order):
    length = row.shape[1]
    source = lax.broadcasted_iota(jnp.int32, (length, length), 0)
    chosen = jnp.where(source == order, 1.0, 0.0).astype(jnp.bfloat16)
    rows = jnp.broadcast_to(row.astype(jnp.float32), (8, length)).astype(jnp.bfloat16)
    return jnp.dot(rows, chosen, preferred_element_type=jnp.float32)[0:1, :].astype(jnp.int32)


def halves(values):
    high = values.astype(jnp.bfloat16)
    low = (values - high.astype(jnp.float32)).astype(jnp.bfloat16)
    return high, low


def blend_kernel(order, steps, fragments, ranks, counts, out, pixels, layers, counted, mixed, *sems):
    owners = order.shape[0]
    capacity = counts.shape[0]
    width = out.shape[1]
    share = owners // steps

    def chunk(source, target, sem, rows, step):
        return pltpu.make_async_copy(source.at[pl.ds(step * rows, rows)], target.at[pl.ds(step * rows, rows)], sem.at[step])

    def copies(step):
        return (
            chunk(ranks, layers, sems[1], share * capacity * 4, step),
            chunk(fragments, pixels, sems[2], share * capacity * 16, step),
        )

    count_copy = pltpu.make_async_copy(counts, counted, sems[0])
    count_copy.start()
    for step in range(steps):
        for copy in copies(step):
            copy.start()
    count_copy.wait()
    pixel = lax.broadcasted_iota(jnp.int32, (owners, width), 1).astype(jnp.float32)
    visible = [
        jnp.where(pixel < columns(counted[slot : slot + 1, :], owners, width), 1.0, 0.0) for slot in range(capacity)
    ]
    for step in range(steps):
        for copy in copies(step):
            copy.wait()
        for slot in range(capacity):
            rank = [
                layers[pl.ds(step * share * capacity * 4 + slot * 4 + layer, share, stride=capacity * 4), :]
                for layer in range(4)
            ]
            entry = [
                [
                    pixels[
                        pl.ds(
                            step * share * capacity * 16 + slot * 16 + layer * 4 + part, share, stride=capacity * 16
                        ),
                        :,
                    ]
                    for part in range(4)
                ]
                for layer in range(4)
            ]
            clear = [1.0 - entry[layer][3] for layer in range(4)]
            weight = [visible[slot][step * share : (step + 1) * share]] * 4
            for one in range(4):
                for two in range(one + 1, 4):
                    ahead = rank[one] < rank[two]
                    weight[two] = weight[two] * jnp.where(ahead, clear[one], 1.0)
                    weight[one] = weight[one] * jnp.where(ahead, 1.0, clear[two])
            for part in range(4):
                total = entry[0][part] * weight[0]
                for layer in range(1, 4):
                    total = total + entry[layer][part] * weight[layer]
                mixed[pl.ds(step * share * capacity * 4 + slot * 4 + part, share, stride=capacity * 4), :] = total
    rows = capacity * 4
    for place, owner in enumerate(order):
        out[pl.ds(place * rows, rows), :] = mixed[pl.ds(int(owner) * rows, rows), :]


def blend(fragments, ranks, counts, order, steps):
    owners, capacity, _, width = fragments.shape
    rows = owners * capacity

    def kernel(*refs):
        blend_kernel(order, steps, *refs)

    return pl.pallas_call(
        kernel,
        in_specs=[pl.BlockSpec(memory_space=pl.ANY)] * 3,
        out_specs=pl.BlockSpec(memory_space=pltpu.VMEM),
        out_shape=pltpu.VMEM((rows * 4, width), jnp.float32),
        scratch_shapes=[
            pltpu.VMEM((rows * 16, width), jnp.float32),
            pltpu.VMEM((rows * 4, width), jnp.int32),
            pltpu.VMEM((capacity, owners), jnp.int32),
            pltpu.VMEM((rows * 4, width), jnp.float32),
            pltpu.SemaphoreType.DMA,
            pltpu.SemaphoreType.DMA((steps,)),
            pltpu.SemaphoreType.DMA((steps,)),
        ],
        name="blend",
    )(fragments.reshape(rows * 16, width), ranks.reshape(rows * 4, width), counts)


def plan_kernel(counts, runs, order, interlace, placed, earlier, target):
    capacity, bricks = runs.shape
    slots = interlace.shape[1]
    total = capacity * bricks
    place = placed[...]
    count = reorder(counts[...], place)
    rank = jnp.concatenate([reorder(order[...], place)] * capacity, axis=1)
    run = jnp.concatenate([reorder(runs[slot : slot + 1, :], place) for slot in range(capacity)], axis=1)
    live = jnp.concatenate([jnp.where(count > slot, 1, 0) for slot in range(capacity)], axis=1) > 0
    run_of = columns(run, total, total).astype(jnp.int32)
    rank_of = columns(rank, total, total).astype(jnp.int32)
    ahead = (run_of == run) & (rank < rank_of) & live
    earlier[...] = jnp.where(ahead, 1.0, 0.0).astype(jnp.bfloat16)
    slot_id = lax.broadcasted_iota(jnp.int32, (slots, total), 0)
    landing = jnp.where(slot_id == run, 1.0, 0.0).astype(jnp.bfloat16)
    screen = jnp.dot(
        jnp.broadcast_to(interlace[...].astype(jnp.float32), (8, slots)).astype(jnp.bfloat16),
        landing,
        preferred_element_type=jnp.float32,
    )[0:1, :].astype(jnp.int32)
    target[...] = jnp.where((slot_id == screen) & live, 1.0, 0.0).astype(jnp.bfloat16)


def plan(counts, runs, order, interlace, placed):
    capacity, bricks = runs.shape
    total = capacity * bricks
    slots = interlace.shape[1]
    return pl.pallas_call(
        plan_kernel,
        out_specs=(pl.BlockSpec(memory_space=pltpu.VMEM),) * 2,
        out_shape=(
            pltpu.VMEM((total, total), jnp.bfloat16),
            pltpu.VMEM((slots, total), jnp.bfloat16),
        ),
        name="plan",
    )(counts, runs, order, interlace, placed)


def strip_kernel(capacity, blocks, earlier, target, out):
    bricks = blocks.shape[0] // (capacity * 4)
    tiles, _, share, width = out.shape

    def part_of(part):
        return jnp.concatenate(
            [blocks[pl.ds(slot * 4 + part, bricks, stride=capacity * 4), :] for slot in range(capacity)],
            axis=0,
        )

    def picked(matrix, values):
        high, low = halves(values)
        return jnp.dot(matrix, high, preferred_element_type=jnp.float32) + jnp.dot(
            matrix, low, preferred_element_type=jnp.float32
        )

    alpha = part_of(3)
    passed = jnp.exp(picked(earlier[...], jnp.log(1.0 - alpha)))
    shaded = jnp.concatenate([part_of(0) * passed, part_of(1) * passed, part_of(2) * passed, alpha * passed], axis=1)
    strip = picked(target[...], shaded)
    for tile in range(tiles):
        for part in range(4):
            out[tile, part] = strip[tile * share : (tile + 1) * share, part * width : (part + 1) * width]


def compose_strip(blocks, earlier, target, capacity, tiles):
    width = blocks.shape[1]
    slots = target.shape[0]

    def kernel(*refs):
        strip_kernel(capacity, *refs)

    return pl.pallas_call(
        kernel,
        in_specs=[pl.BlockSpec(memory_space=pltpu.VMEM)] * 3,
        out_specs=pl.BlockSpec(memory_space=pltpu.VMEM),
        out_shape=pltpu.VMEM((tiles, 4, slots // tiles, width), jnp.float32),
        name="strip",
    )(resident(blocks), resident(earlier), resident(target))


def stack_kernel(strips, out):
    slabs, _, share, _ = strips.shape
    total = [strips[slabs - 1, part] for part in range(4)]
    for slab in range(slabs - 2, -1, -1):
        clear = 1.0 - strips[slab, 3]
        total = [strips[slab, part] + clear * total[part] for part in range(4)]
    for part in range(4):
        out[pl.ds(part, share, stride=4), :] = total[part]


def stack(strips):
    _, _, share, width = strips.shape
    return pl.pallas_call(
        stack_kernel,
        in_specs=[pl.BlockSpec(memory_space=pltpu.VMEM)],
        out_shape=jax.ShapeDtypeStruct((share * 4, width), jnp.float32),
        name="stack",
    )(resident(strips))


def exchange_order(tiles, bricks):
    return np.array(
        [
            (tile + tiles // 2 + 1) % tiles * bricks + (brick + tile + bricks // 2) % bricks
            for brick in range(bricks)
            for tile in range(tiles)
        ],
        np.int32,
    )


def shards(fragments, layer_rank, pixel_count, slot_count, block_run, brick_order, interlace):
    _, _, owners, capacity, _, width = fragments.shape
    slots = interlace.shape[0]
    tiles = lax.axis_size("depth")
    order = exchange_order(lax.axis_size("tile"), lax.axis_size("brick"))
    blocks = blend(fragments[0, 0], layer_rank[0, 0], pixel_count[0, 0].T, order, 4)
    sent = lax.all_to_all(
        blocks.reshape(owners, capacity * 4, width),
        ("tile", "brick"),
        split_axis=0,
        concat_axis=0,
        tiled=True,
        axis_index_groups=[order.tolist()],
    )
    earlier, target = plan(
        slot_count[0], block_run[0, 0].T, brick_order, interlace.reshape(1, slots), jnp.asarray(order).reshape(1, owners)
    )
    strip = compose_strip(sent.reshape(owners * capacity * 4, width), earlier, target, capacity, tiles)
    strips = lax.all_to_all(strip, "depth", split_axis=0, concat_axis=0, tiled=True)
    return stack(strips).reshape(1, 1, slots // tiles, 4, width)


def solution(mesh):
    return jax.shard_map(
        shards,
        mesh=mesh,
        in_specs=(
            P("depth", ("tile", "brick"), None, None, None, None),
            P("depth", ("tile", "brick"), None, None, None),
            P("depth", ("tile", "brick"), None, None),
            P("depth", ("tile", "brick"), None),
            P("depth", ("tile", "brick"), None, None),
            P("depth", None),
            P(),
        ),
        out_specs=P(("tile", "brick"), "depth", None, None, None),
        check_vma=False,
    )
```

```python
import jax
import jax.numpy as jnp
import numpy as np
from jax import lax
from jax.experimental import pallas as pl
from jax.experimental.pallas import tpu as pltpu
from jax.sharding import PartitionSpec as P


def resident(array):
    return pltpu.with_memory_space_constraint(array, pltpu.VMEM)


def columns(row, rows, width):
    length = row.shape[1]
    place = lax.broadcasted_iota(jnp.int32, (rows, length), 1)
    own = lax.broadcasted_iota(jnp.int32, (rows, length), 0)
    spread = jnp.where(place == own, row.astype(jnp.float32), 0.0).astype(jnp.bfloat16)
    return jnp.dot(spread, jnp.ones((length, width), jnp.bfloat16), preferred_element_type=jnp.float32)


def reorder(row, order):
    length = row.shape[1]
    source = lax.broadcasted_iota(jnp.int32, (length, length), 0)
    chosen = jnp.where(source == order, 1.0, 0.0).astype(jnp.bfloat16)
    rows = jnp.broadcast_to(row.astype(jnp.float32), (8, length)).astype(jnp.bfloat16)
    return jnp.dot(rows, chosen, preferred_element_type=jnp.float32)[0:1, :].astype(jnp.int32)


def halves(values):
    high = values.astype(jnp.bfloat16)
    low = (values - high.astype(jnp.float32)).astype(jnp.bfloat16)
    return high, low


def picked(matrix, values):
    high, low = halves(values)
    return jnp.dot(matrix, high, preferred_element_type=jnp.float32) + jnp.dot(
        matrix, low, preferred_element_type=jnp.float32
    )


def turned(values):
    return pltpu.roll(values, values.shape[-1] // 2, values.ndim - 1)


def in_left(values):
    lane = lax.broadcasted_iota(jnp.int32, values.shape, values.ndim - 1)
    return lane < values.shape[-1] // 2


def lefts(one, two):
    return jnp.where(in_left(one), one, turned(two))


def rights(one, two):
    return jnp.where(in_left(one), turned(one), two)


def blend_kernel(root, steps, fragments, ranks, counts, out, pixels, layers, counted, *sems):
    capacity, owners = counts.shape
    width = out.shape[1]
    share = owners // steps

    def chunk(source, target, sem, rows, step):
        return pltpu.make_async_copy(source.at[pl.ds(step * rows, rows)], target.at[pl.ds(step * rows, rows)], sem.at[step])

    def copies(step):
        return (
            chunk(ranks, layers, sems[1], share * capacity * 4, step),
            chunk(fragments, pixels, sems[2], share * capacity * 16, step),
        )

    count_copy = pltpu.make_async_copy(counts, counted, sems[0])
    count_copy.start()
    for step in range(steps):
        for copy in copies(step):
            copy.start()
    count_copy.wait()
    pixel = lax.broadcasted_iota(jnp.int32, (owners, width), 1).astype(jnp.float32)
    visible = [
        jnp.where(pixel < columns(counted[slot : slot + 1, :], owners, width), 1.0, 0.0) for slot in range(capacity)
    ]
    for step in range(steps):
        for copy in copies(step):
            copy.wait()
        blended = []
        for slot in range(capacity):
            rank = [
                layers[pl.ds(step * share * capacity * 4 + slot * 4 + layer, share, stride=capacity * 4), :]
                for layer in range(4)
            ]
            entry = [
                [
                    pixels[
                        pl.ds(
                            step * share * capacity * 16 + slot * 16 + layer * 4 + part, share, stride=capacity * 16
                        ),
                        :,
                    ]
                    for part in range(4)
                ]
                for layer in range(4)
            ]
            clear = [1.0 - entry[layer][3] for layer in range(4)]
            weight = [visible[slot][step * share : (step + 1) * share]] * 4
            for one in range(4):
                for two in range(one + 1, 4):
                    ahead = rank[one] < rank[two]
                    weight[two] = weight[two] * jnp.where(ahead, clear[one], 1.0)
                    weight[one] = weight[one] * jnp.where(ahead, 1.0, clear[two])
            mixed = []
            for part in range(4):
                total = entry[0][part] * weight[0]
                for layer in range(1, 4):
                    total = total + entry[layer][part] * weight[layer]
                mixed.append(total)
            blended.append(mixed)
        for part in range(4):
            one, two = blended[0][part], blended[1][part]
            out[pl.ds(step * share * 4 + part, share, stride=4), :] = rights(one, two)
            out[pl.ds((owners + step * share) * 4 + part, share, stride=4), :] = lefts(one, two)
    for half in range(2):
        first = pl.ds(half * owners * 4, 4)
        other = pl.ds((half * owners + root) * 4, 4)
        moved = out[first, :]
        out[first, :] = out[other, :]
        out[other, :] = moved


def blend(fragments, ranks, counts, root, steps):
    owners, capacity, _, width = fragments.shape
    rows = owners * capacity

    def kernel(*refs):
        blend_kernel(root, steps, *refs)

    return pl.pallas_call(
        kernel,
        in_specs=[pl.BlockSpec(memory_space=pl.ANY)] * 3,
        out_specs=pl.BlockSpec(memory_space=pltpu.VMEM),
        out_shape=jax.ShapeDtypeStruct((rows * 4, width), jnp.float32),
        scratch_shapes=[
            pltpu.VMEM((rows * 16, width), jnp.float32),
            pltpu.VMEM((rows * 4, width), jnp.int32),
            pltpu.VMEM((capacity, owners), jnp.int32),
            pltpu.SemaphoreType.DMA,
            pltpu.SemaphoreType.DMA((steps,)),
            pltpu.SemaphoreType.DMA((steps,)),
        ],
        name="blend",
    )(fragments.reshape(rows * 16, width), ranks.reshape(rows * 4, width), counts)


def plan_kernel(capacity, index, interlace, placed, earlier, target):
    bricks = placed.shape[1]
    slots = interlace.shape[1]
    total = capacity * bricks
    place = placed[...]
    for slab in range(2):
        count = reorder(index[slab, 0:1, :], place)
        rank = jnp.concatenate([reorder(index[slab, 1:2, :], place)] * capacity, axis=1)
        run = jnp.concatenate(
            [reorder(index[slab, 2 + slot : 3 + slot, :], place) for slot in range(capacity)], axis=1
        )
        live = jnp.concatenate([jnp.where(count > slot, 1, 0) for slot in range(capacity)], axis=1) > 0
        run_of = columns(run, total, total).astype(jnp.int32)
        rank_of = columns(rank, total, total).astype(jnp.int32)
        ahead = (run_of == run) & (rank < rank_of) & live
        earlier[:, slab * total : (slab + 1) * total] = jnp.where(ahead, 1.0, 0.0).astype(jnp.bfloat16)
        slot_id = lax.broadcasted_iota(jnp.int32, (slots, total), 0)
        landing = jnp.where(slot_id == run, 1.0, 0.0).astype(jnp.bfloat16)
        screen = jnp.dot(
            jnp.broadcast_to(interlace[...].astype(jnp.float32), (8, slots)).astype(jnp.bfloat16),
            landing,
            preferred_element_type=jnp.float32,
        )[0:1, :].astype(jnp.int32)
        target[:, slab * total : (slab + 1) * total] = jnp.where((slot_id == screen) & live, 1.0, 0.0).astype(
            jnp.bfloat16
        )


def plan(index, interlace, placed, capacity):
    total = capacity * placed.shape[1]
    slots = interlace.shape[1]

    def kernel(*refs):
        plan_kernel(capacity, *refs)

    return pl.pallas_call(
        kernel,
        out_specs=(pl.BlockSpec(memory_space=pltpu.VMEM),) * 2,
        out_shape=(
            pltpu.VMEM((total, 2 * total), jnp.bfloat16),
            pltpu.VMEM((slots, 2 * total), jnp.bfloat16),
        ),
        name="plan",
    )(index, interlace, placed)


def strip_kernel(blocks, earlier, target, out):
    bricks = blocks.shape[0] // 8
    tiles, _, share, width = out.shape

    def part_of(part):
        back = blocks[pl.ds(part, bricks, stride=4), :]
        front = blocks[pl.ds(bricks * 4 + part, bricks, stride=4), :]
        return jnp.concatenate([lefts(front, back), rights(front, back)], axis=0)

    def apart(values):
        left = in_left(values)
        return jnp.concatenate([jnp.where(left, values, 0.0), jnp.where(left, 0.0, values)], axis=0)

    parts = [part_of(part) for part in range(4)]
    passed = jnp.exp(picked(earlier[...], apart(jnp.log(1.0 - parts[3]))))
    shaded = jnp.concatenate([apart(part * passed) for part in parts], axis=1)
    strip = picked(target[...], shaded)
    strips = [strip[:, part * width : (part + 1) * width] for part in range(4)]
    clear = 1.0 - lefts(strips[3], strips[3])
    for pair in range(2):
        one, two = strips[2 * pair], strips[2 * pair + 1]
        merged = lefts(one, two) + clear * rights(one, two)
        for tile in range(tiles):
            out[tile, pair] = merged[tile * share : (tile + 1) * share]


def compose_strip(blocks, earlier, target, tiles):
    width = blocks.shape[1]
    slots = target.shape[0]
    return pl.pallas_call(
        strip_kernel,
        in_specs=[pl.BlockSpec(memory_space=pltpu.VMEM)] * 3,
        out_specs=pl.BlockSpec(memory_space=pltpu.VMEM),
        out_shape=pltpu.VMEM((tiles, 2, slots // tiles, width), jnp.float32),
        name="strip",
    )(resident(blocks), resident(earlier), resident(target))


def stack_kernel(strips, out):
    slabs, _, share, _ = strips.shape
    totals = []
    for half in range(2):
        total = [strips[slabs - 2 + half, pair] for pair in range(2)]
        for slab in range(slabs - 4, -1, -2):
            front = [strips[slab + half, pair] for pair in range(2)]
            clear = 1.0 - jnp.where(in_left(front[1]), turned(front[1]), front[1])
            total = [front[pair] + clear * total[pair] for pair in range(2)]
        totals.append(total)
    for pair in range(2):
        out[pl.ds(2 * pair, share, stride=4), :] = lefts(totals[0][pair], totals[1][pair])
        out[pl.ds(2 * pair + 1, share, stride=4), :] = rights(totals[0][pair], totals[1][pair])


def stack(strips):
    _, _, share, width = strips.shape
    return pl.pallas_call(
        stack_kernel,
        in_specs=[pl.BlockSpec(memory_space=pltpu.VMEM)],
        out_shape=jax.ShapeDtypeStruct((share * 4, width), jnp.float32),
        name="stack",
    )(resident(strips))


def shards(fragments, layer_rank, pixel_count, slot_count, block_run, brick_order, interlace):
    _, _, owners, capacity, _, width = fragments.shape
    slots = interlace.shape[0]
    tiles = lax.axis_size("depth")
    bricks = lax.axis_size("brick")
    root = (lax.axis_size("tile") // 2 + 1) * bricks + bricks // 2
    order = np.arange(owners, dtype=np.int32)
    order[0], order[root] = root, 0
    blocks = blend(fragments[0, 0], layer_rank[0, 0], pixel_count[0, 0].T, root, 4)
    groups = [
        [int(owners * (2 * chip + core) + owner) for core in (1, 0) for owner in order] for chip in range(tiles // 2)
    ]
    sent = lax.all_to_all(
        blocks.reshape(2 * owners, 4, width),
        ("depth", "tile", "brick"),
        split_axis=0,
        concat_axis=0,
        tiled=True,
        axis_index_groups=groups,
    )
    own = jnp.concatenate([slot_count[0], brick_order, block_run[0, 0].T], axis=0)
    other = lax.ppermute(own, "depth", [(place, place ^ 1) for place in range(tiles)])
    in_front = lax.axis_index("depth") % 2 == 0
    index = jnp.stack([jnp.where(in_front, own, other), jnp.where(in_front, other, own)])
    earlier, target = plan(index, interlace.reshape(1, slots), jnp.asarray(order).reshape(1, owners), capacity)
    strip = compose_strip(sent.reshape(owners * 8, width), earlier, target, tiles)
    strips = lax.all_to_all(strip, "depth", split_axis=0, concat_axis=0, tiled=True)
    return stack(strips).reshape(1, 1, slots // tiles, 4, width)


def solution(mesh):
    return jax.shard_map(
        shards,
        mesh=mesh,
        in_specs=(
            P("depth", ("tile", "brick"), None, None, None, None),
            P("depth", ("tile", "brick"), None, None, None),
            P("depth", ("tile", "brick"), None, None),
            P("depth", ("tile", "brick"), None),
            P("depth", ("tile", "brick"), None, None),
            P("depth", None),
            P(),
        ),
        out_specs=P(("tile", "brick"), "depth", None, None, None),
        check_vma=False,
    )
```

```python
import jax
import jax.numpy as jnp
import numpy as np
from jax import lax
from jax.experimental import pallas as pl
from jax.experimental.pallas import tpu as pltpu
from jax.sharding import PartitionSpec as P


def resident(array):
    return pltpu.with_memory_space_constraint(array, pltpu.VMEM)


def columns(row, rows, width):
    length = row.shape[1]
    place = lax.broadcasted_iota(jnp.int32, (rows, length), 1)
    own = lax.broadcasted_iota(jnp.int32, (rows, length), 0)
    spread = jnp.where(place == own, row.astype(jnp.float32), 0.0).astype(jnp.bfloat16)
    return jnp.dot(spread, jnp.ones((length, width), jnp.bfloat16), preferred_element_type=jnp.float32)


def reorder(row, order):
    length = row.shape[1]
    source = lax.broadcasted_iota(jnp.int32, (length, length), 0)
    chosen = jnp.where(source == order, 1.0, 0.0).astype(jnp.bfloat16)
    rows = jnp.broadcast_to(row.astype(jnp.float32), (8, length)).astype(jnp.bfloat16)
    return jnp.dot(rows, chosen, preferred_element_type=jnp.float32)[0:1, :].astype(jnp.int32)


def halves(values):
    high = values.astype(jnp.bfloat16)
    low = (values - high.astype(jnp.float32)).astype(jnp.bfloat16)
    return high, low


def picked(matrix, values):
    high, low = halves(values)
    return jnp.dot(matrix, high, preferred_element_type=jnp.float32) + jnp.dot(
        matrix, low, preferred_element_type=jnp.float32
    )


def turned(values):
    return pltpu.roll(values, values.shape[-1] // 2, values.ndim - 1)


def in_left(values):
    lane = lax.broadcasted_iota(jnp.int32, values.shape, values.ndim - 1)
    return lane < values.shape[-1] // 2


def lefts(one, two):
    return jnp.where(in_left(one), one, turned(two))


def rights(one, two):
    return jnp.where(in_left(one), turned(one), two)


def blend_kernel(root, steps, fragments, ranks, counts, out, pixels, layers, counted, *sems):
    capacity, owners = counts.shape
    width = out.shape[1]
    share = owners // steps

    def chunk(source, target, sem, rows, step):
        return pltpu.make_async_copy(source.at[pl.ds(step * rows, rows)], target.at[pl.ds(step * rows, rows)], sem.at[step])

    def copies(step):
        return (
            chunk(ranks, layers, sems[1], share * capacity * 4, step),
            chunk(fragments, pixels, sems[2], share * capacity * 16, step),
        )

    count_copy = pltpu.make_async_copy(counts, counted, sems[0])
    count_copy.start()
    for step in range(steps):
        for copy in copies(step):
            copy.start()
    count_copy.wait()
    pixel = lax.broadcasted_iota(jnp.int32, (owners, width), 1).astype(jnp.float32)
    visible = [
        jnp.where(pixel < columns(counted[slot : slot + 1, :], owners, width), 1.0, 0.0) for slot in range(capacity)
    ]
    for step in range(steps):
        for copy in copies(step):
            copy.wait()
        blended = []
        for slot in range(capacity):
            rank = [
                layers[pl.ds(step * share * capacity * 4 + slot * 4 + layer, share, stride=capacity * 4), :]
                for layer in range(4)
            ]
            entry = [
                [
                    pixels[
                        pl.ds(
                            step * share * capacity * 16 + slot * 16 + layer * 4 + part, share, stride=capacity * 16
                        ),
                        :,
                    ]
                    for part in range(4)
                ]
                for layer in range(4)
            ]
            clear = [1.0 - entry[layer][3] for layer in range(4)]
            weight = [visible[slot][step * share : (step + 1) * share]] * 4
            for one in range(4):
                for two in range(one + 1, 4):
                    ahead = rank[one] < rank[two]
                    weight[two] = weight[two] * jnp.where(ahead, clear[one], 1.0)
                    weight[one] = weight[one] * jnp.where(ahead, 1.0, clear[two])
            mixed = []
            for part in range(4):
                total = entry[0][part] * weight[0]
                for layer in range(1, 4):
                    total = total + entry[layer][part] * weight[layer]
                mixed.append(total)
            blended.append(mixed)
        for part in range(4):
            one, two = blended[0][part], blended[1][part]
            out[pl.ds(step * share * 4 + part, share, stride=4), :] = rights(one, two)
            out[pl.ds((owners + step * share) * 4 + part, share, stride=4), :] = lefts(one, two)
    for half in range(2):
        first = pl.ds(half * owners * 4, 4)
        other = pl.ds((half * owners + root) * 4, 4)
        moved = out[first, :]
        out[first, :] = out[other, :]
        out[other, :] = moved


def blend(fragments, ranks, counts, root, steps):
    owners, capacity, _, width = fragments.shape
    rows = owners * capacity

    def kernel(*refs):
        blend_kernel(root, steps, *refs)

    return pl.pallas_call(
        kernel,
        in_specs=[pl.BlockSpec(memory_space=pl.ANY)] * 3,
        out_specs=pl.BlockSpec(memory_space=pltpu.VMEM),
        out_shape=jax.ShapeDtypeStruct((rows * 4, width), jnp.float32),
        scratch_shapes=[
            pltpu.VMEM((rows * 16, width), jnp.float32),
            pltpu.VMEM((rows * 4, width), jnp.int32),
            pltpu.VMEM((capacity, owners), jnp.int32),
            pltpu.SemaphoreType.DMA,
            pltpu.SemaphoreType.DMA((steps,)),
            pltpu.SemaphoreType.DMA((steps,)),
        ],
        name="blend",
    )(fragments.reshape(rows * 16, width), ranks.reshape(rows * 4, width), counts)


def plan_kernel(capacity, index, interlace, placed, earlier, target):
    bricks = placed.shape[1]
    slots = interlace.shape[1]
    total = capacity * bricks
    place = placed[...]
    for slab in range(2):
        count = reorder(index[slab, 0:1, :], place)
        rank = jnp.concatenate([reorder(index[slab, 1:2, :], place)] * capacity, axis=1)
        run = jnp.concatenate(
            [reorder(index[slab, 2 + slot : 3 + slot, :], place) for slot in range(capacity)], axis=1
        )
        live = jnp.concatenate([jnp.where(count > slot, 1, 0) for slot in range(capacity)], axis=1) > 0
        run_of = columns(run, total, total).astype(jnp.int32)
        rank_of = columns(rank, total, total).astype(jnp.int32)
        ahead = (run_of == run) & (rank < rank_of) & live
        earlier[:, slab * total : (slab + 1) * total] = jnp.where(ahead, 1.0, 0.0).astype(jnp.bfloat16)
        slot_id = lax.broadcasted_iota(jnp.int32, (slots, total), 0)
        landing = jnp.where(slot_id == run, 1.0, 0.0).astype(jnp.bfloat16)
        screen = jnp.dot(
            jnp.broadcast_to(interlace[...].astype(jnp.float32), (8, slots)).astype(jnp.bfloat16),
            landing,
            preferred_element_type=jnp.float32,
        )[0:1, :].astype(jnp.int32)
        target[:, slab * total : (slab + 1) * total] = jnp.where((slot_id == screen) & live, 1.0, 0.0).astype(
            jnp.bfloat16
        )


def plan(index, interlace, placed, capacity):
    total = capacity * placed.shape[1]
    slots = interlace.shape[1]

    def kernel(*refs):
        plan_kernel(capacity, *refs)

    return pl.pallas_call(
        kernel,
        out_specs=(pl.BlockSpec(memory_space=pltpu.VMEM),) * 2,
        out_shape=(
            pltpu.VMEM((total, 2 * total), jnp.bfloat16),
            pltpu.VMEM((slots, 2 * total), jnp.bfloat16),
        ),
        name="plan",
    )(index, interlace, placed)


def strip_kernel(first, blocks, earlier, target, out):
    bricks = blocks.shape[0] // 8
    tiles, _, share, width = out.shape

    def part_of(part):
        back = blocks[pl.ds(part, bricks, stride=4), :]
        front = blocks[pl.ds(bricks * 4 + part, bricks, stride=4), :]
        return jnp.concatenate([lefts(front, back), rights(front, back)], axis=0)

    def apart(values):
        left = in_left(values)
        return jnp.concatenate([jnp.where(left, values, 0.0), jnp.where(left, 0.0, values)], axis=0)

    parts = [part_of(part) for part in range(4)]
    passed = jnp.exp(picked(earlier[...], apart(jnp.log(1.0 - parts[3]))))
    shaded = jnp.concatenate([apart(part * passed) for part in parts], axis=1)
    strip = picked(target[...], shaded)
    strips = [strip[:, part * width : (part + 1) * width] for part in range(4)]
    clear = 1.0 - lefts(strips[3], strips[3])
    for pair in range(2):
        one, two = strips[2 * pair], strips[2 * pair + 1]
        merged = lefts(one, two) + clear * rights(one, two)
        for tile in range(tiles):
            out[tile ^ first, pair] = merged[tile * share : (tile + 1) * share]


def compose_strip(blocks, earlier, target, tiles, first):
    width = blocks.shape[1]
    slots = target.shape[0]

    def kernel(*refs):
        strip_kernel(first, *refs)

    return pl.pallas_call(
        kernel,
        in_specs=[pl.BlockSpec(memory_space=pltpu.VMEM)] * 3,
        out_specs=pl.BlockSpec(memory_space=pltpu.VMEM),
        out_shape=pltpu.VMEM((tiles, 2, slots // tiles, width), jnp.float32),
        name="strip",
    )(resident(blocks), resident(earlier), resident(target))


def stack_kernel(first, strips, out):
    slabs, _, share, _ = strips.shape
    totals = []
    for half in range(2):
        total = [strips[(slabs - 2 + half) ^ first, pair] for pair in range(2)]
        for slab in range(slabs - 4, -1, -2):
            front = [strips[(slab + half) ^ first, pair] for pair in range(2)]
            clear = 1.0 - jnp.where(in_left(front[1]), turned(front[1]), front[1])
            total = [front[pair] + clear * total[pair] for pair in range(2)]
        totals.append(total)
    for pair in range(2):
        out[pl.ds(2 * pair, share, stride=4), :] = lefts(totals[0][pair], totals[1][pair])
        out[pl.ds(2 * pair + 1, share, stride=4), :] = rights(totals[0][pair], totals[1][pair])


def stack(strips, first):
    _, _, share, width = strips.shape

    def kernel(*refs):
        stack_kernel(first, *refs)

    return pl.pallas_call(
        kernel,
        in_specs=[pl.BlockSpec(memory_space=pltpu.VMEM)],
        out_shape=jax.ShapeDtypeStruct((share * 4, width), jnp.float32),
        name="stack",
    )(resident(strips))


def shards(fragments, layer_rank, pixel_count, slot_count, block_run, brick_order, interlace):
    _, _, owners, capacity, _, width = fragments.shape
    slots = interlace.shape[0]
    tiles = lax.axis_size("depth")
    bricks = lax.axis_size("brick")
    first = tiles // 2 + 1
    root = (lax.axis_size("tile") // 2 + 1) * bricks + bricks // 2
    order = np.arange(owners, dtype=np.int32)
    order[0], order[root] = root, 0
    blocks = blend(fragments[0, 0], layer_rank[0, 0], pixel_count[0, 0].T, root, 4)
    groups = [
        [int(owners * (2 * chip + core) + owner) for core in (1, 0) for owner in order] for chip in range(tiles // 2)
    ]
    sent = lax.all_to_all(
        blocks.reshape(2 * owners, 4, width),
        ("depth", "tile", "brick"),
        split_axis=0,
        concat_axis=0,
        tiled=True,
        axis_index_groups=groups,
    )
    own = jnp.concatenate([slot_count[0], brick_order, block_run[0, 0].T], axis=0)
    other = lax.ppermute(own, "depth", [(place, place ^ 1) for place in range(tiles)])
    in_front = lax.axis_index("depth") % 2 == 0
    index = jnp.stack([jnp.where(in_front, own, other), jnp.where(in_front, other, own)])
    earlier, target = plan(index, interlace.reshape(1, slots), jnp.asarray(order).reshape(1, owners), capacity)
    strip = compose_strip(sent.reshape(owners * 8, width), earlier, target, tiles, first)
    strips = lax.all_to_all(
        strip,
        "depth",
        split_axis=0,
        concat_axis=0,
        tiled=True,
        axis_index_groups=[[place ^ first for place in range(tiles)]],
    )
    return stack(strips, first).reshape(1, 1, slots // tiles, 4, width)


def solution(mesh):
    return jax.shard_map(
        shards,
        mesh=mesh,
        in_specs=(
            P("depth", ("tile", "brick"), None, None, None, None),
            P("depth", ("tile", "brick"), None, None, None),
            P("depth", ("tile", "brick"), None, None),
            P("depth", ("tile", "brick"), None),
            P("depth", ("tile", "brick"), None, None),
            P("depth", None),
            P(),
        ),
        out_specs=P(("tile", "brick"), "depth", None, None, None),
        check_vma=False,
    )
```

```python
import jax
import jax.numpy as jnp
import numpy as np
from jax import lax
from jax.experimental import pallas as pl
from jax.experimental.pallas import tpu as pltpu
from jax.sharding import PartitionSpec as P


def resident(array):
    return pltpu.with_memory_space_constraint(array, pltpu.VMEM)


def columns(row, rows, width):
    length = row.shape[1]
    place = lax.broadcasted_iota(jnp.int32, (rows, length), 1)
    own = lax.broadcasted_iota(jnp.int32, (rows, length), 0)
    spread = jnp.where(place == own, row.astype(jnp.float32), 0.0).astype(jnp.bfloat16)
    return jnp.dot(spread, jnp.ones((length, width), jnp.bfloat16), preferred_element_type=jnp.float32)


def reorder(row, order):
    length = row.shape[1]
    source = lax.broadcasted_iota(jnp.int32, (length, length), 0)
    chosen = jnp.where(source == order, 1.0, 0.0).astype(jnp.bfloat16)
    rows = jnp.broadcast_to(row.astype(jnp.float32), (8, length)).astype(jnp.bfloat16)
    return jnp.dot(rows, chosen, preferred_element_type=jnp.float32)[0:1, :].astype(jnp.int32)


def halves(values):
    high = values.astype(jnp.bfloat16)
    low = (values - high.astype(jnp.float32)).astype(jnp.bfloat16)
    return high, low


def picked(matrix, values):
    return jnp.dot(matrix, jnp.concatenate(halves(values), axis=0), preferred_element_type=jnp.float32)


def turned(values):
    return pltpu.roll(values, values.shape[-1] // 2, values.ndim - 1)


def in_left(values):
    lane = lax.broadcasted_iota(jnp.int32, values.shape, values.ndim - 1)
    return lane < values.shape[-1] // 2


def lefts(one, two):
    return jnp.where(in_left(one), one, turned(two))


def rights(one, two):
    return jnp.where(in_left(one), turned(one), two)


def blend_kernel(root, fragments, ranks, counts, out, pixels, layers, counted, mixed, *sems):
    capacity, owners = counts.shape
    width = out.shape[1]
    share = owners // 2
    pitch = pixels.shape[0] // owners
    wide = share * capacity * 4

    def fetched(step):
        rows = pl.ds(step * share, share)
        place = pixels.reshape(owners, pitch, width).at[rows, pl.ds(0, capacity * 16)]
        return pltpu.make_async_copy(fragments.at[rows], place, sems[0].at[step])

    def stored(step):
        rows = pl.ds((1 - step) * wide, wide)
        return pltpu.make_async_copy(mixed.at[rows], out.at[rows], sems[1].at[step])

    rank_copy = pltpu.make_async_copy(ranks, layers, sems[2])
    count_copy = pltpu.make_async_copy(counts, counted, sems[3])
    fetched(1).start()
    rank_copy.start()
    count_copy.start()
    fetched(0).start()
    pixel = lax.broadcasted_iota(jnp.int32, (owners, width), 1).astype(jnp.float32)
    visible = None
    for step in (1, 0):
        if visible is None:
            rank_copy.wait()
            count_copy.wait()
            visible = [
                jnp.where(pixel < columns(counted[slot : slot + 1, :], owners, width), 1.0, 0.0)
                for slot in range(capacity)
            ]
        fetched(step).wait()
        blended = []
        for slot in range(capacity):
            rank = [
                layers[pl.ds(step * wide + slot * 4 + layer, share, stride=capacity * 4), :] for layer in range(4)
            ]
            entry = [
                [
                    pixels[pl.ds(step * share * pitch + slot * 16 + layer * 4 + part, share, stride=pitch), :]
                    for part in range(4)
                ]
                for layer in range(4)
            ]
            clear = [1.0 - entry[layer][3] for layer in range(4)]
            weight = [visible[slot][step * share : (step + 1) * share]] * 4
            for one in range(4):
                for two in range(one + 1, 4):
                    ahead = rank[one] < rank[two]
                    weight[two] = weight[two] * jnp.where(ahead, clear[one], 1.0)
                    weight[one] = weight[one] * jnp.where(ahead, 1.0, clear[two])
            blended.append([])
            for part in range(4):
                total = entry[0][part] * weight[0]
                for layer in range(1, 4):
                    total = total + entry[layer][part] * weight[layer]
                blended[slot].append(total)
        base = (1 - step) * wide
        for part in range(4):
            one, two = blended[0][part], blended[1][part]
            mixed[pl.ds(base + part, share, stride=4), :] = rights(one, two)
            mixed[pl.ds(base + wide // 2 + part, share, stride=4), :] = lefts(one, two)
        if step == 1:
            for half in range(2):
                first = pl.ds(half * wide // 2, 4)
                other = pl.ds(half * wide // 2 + (root - share) * 4, 4)
                moved = mixed[first, :]
                mixed[first, :] = mixed[other, :]
                mixed[other, :] = moved
        stored(step).start()
    for step in (1, 0):
        stored(step).wait()


def blend(fragments, ranks, counts, root):
    owners, capacity, _, width = fragments.shape
    rows = owners * capacity

    def kernel(*refs):
        blend_kernel(root, *refs)

    return pl.pallas_call(
        kernel,
        in_specs=[pl.BlockSpec(memory_space=pl.ANY)] * 3,
        out_specs=pl.BlockSpec(memory_space=pl.ANY),
        out_shape=jax.ShapeDtypeStruct((rows * 4, width), jnp.float32),
        scratch_shapes=[
            pltpu.VMEM((owners * (capacity * 16 + 8), width), jnp.float32),
            pltpu.VMEM((rows * 4, width), jnp.int32),
            pltpu.VMEM((capacity, owners), jnp.int32),
            pltpu.VMEM((rows * 4, width), jnp.float32),
            pltpu.SemaphoreType.DMA((2,)),
            pltpu.SemaphoreType.DMA((2,)),
            pltpu.SemaphoreType.DMA,
            pltpu.SemaphoreType.DMA,
        ],
        name="blend",
    )(fragments.reshape(owners, capacity * 16, width), ranks.reshape(rows * 4, width), counts)


def plan_kernel(capacity, tiles, index, interlace, placed, earlier, plain, crossed):
    bricks = placed.shape[1]
    slots = interlace.shape[1]
    total = capacity * bricks
    place = placed[...]
    gap = slots // tiles // 2
    row = lax.broadcasted_iota(jnp.int32, (slots // 2, total), 0)
    near = row + row // gap * gap

    def store(target, slab, chosen):
        ones = jnp.where(chosen, 1.0, 0.0).astype(jnp.bfloat16)
        rows = ones.shape[0]
        target[slab * rows : (slab + 1) * rows, :] = jnp.concatenate([ones, ones], axis=1)

    for slab in range(2):
        count = reorder(index[slab, 0:1, :], place)
        rank = jnp.concatenate([reorder(index[slab, 1:2, :], place)] * capacity, axis=1)
        run = jnp.concatenate(
            [reorder(index[slab, 2 + slot : 3 + slot, :], place) for slot in range(capacity)], axis=1
        )
        live = jnp.concatenate([jnp.where(count > slot, 1, 0) for slot in range(capacity)], axis=1) > 0
        run_of = columns(run, total, total).astype(jnp.int32)
        rank_of = columns(rank, total, total).astype(jnp.int32)
        store(earlier, slab, (run_of == run) & (rank < rank_of) & live)
        slot_id = lax.broadcasted_iota(jnp.int32, (slots, total), 0)
        landing = jnp.where(slot_id == run, 1.0, 0.0).astype(jnp.bfloat16)
        screen = jnp.dot(
            jnp.broadcast_to(interlace[...].astype(jnp.float32), (8, slots)).astype(jnp.bfloat16),
            landing,
            preferred_element_type=jnp.float32,
        )[0:1, :].astype(jnp.int32)
        store((plain, crossed)[slab], slab, (near == screen) & live)
        store((crossed, plain)[slab], slab, (near + gap == screen) & live)


def plan(index, interlace, placed, capacity, tiles):
    total = capacity * placed.shape[1]
    slots = interlace.shape[1]

    def kernel(*refs):
        plan_kernel(capacity, tiles, *refs)

    return pl.pallas_call(
        kernel,
        out_specs=(pl.BlockSpec(memory_space=pltpu.VMEM),) * 3,
        out_shape=(
            pltpu.VMEM((2 * total, 2 * total), jnp.bfloat16),
            pltpu.VMEM((slots, 2 * total), jnp.bfloat16),
            pltpu.VMEM((slots, 2 * total), jnp.bfloat16),
        ),
        name="plan",
    )(index, interlace, placed)


def strip_kernel(first, blocks, earlier, plain, crossed, out):
    tiles, _, share, width = out.shape
    quarter = blocks.shape[0] // 4

    def rows_of(side, part):
        return jnp.concatenate(
            [blocks[pl.ds((2 * run + side) * quarter + part, quarter // 4, stride=4), :] for run in range(2)], axis=0
        )

    def part_of(part):
        front, back = rows_of(1, part), rows_of(0, part)
        return jnp.concatenate([lefts(front, back), rights(front, back)], axis=0)

    def sides(values):
        half = values.shape[0] // 2
        return values[:half], values[half:]

    parts = [part_of(part) for part in range(4)]
    front, back = sides(picked(earlier[...], jnp.log(1.0 - parts[3])))
    passed = jnp.exp(jnp.where(in_left(front), front, back))
    shaded = [part * passed for part in parts]
    here_front, here_back = sides(picked(plain[...], jnp.concatenate(shaded, axis=1)))
    there_front, there_back = sides(picked(crossed[...], jnp.concatenate([turned(part) for part in shaded], axis=1)))
    fronts, backs = [], []
    for part in range(4):
        lanes = slice(part * width, (part + 1) * width)
        left = in_left(here_front[:, lanes])
        fronts.append(jnp.where(left, here_front[:, lanes], there_front[:, lanes]))
        backs.append(jnp.where(left, there_back[:, lanes], here_back[:, lanes]))
    clear = 1.0 - fronts[3]
    for part in range(4):
        merged = fronts[part] + clear * backs[part]
        for tile in range(tiles):
            out[tile ^ first, part] = merged[tile * share : (tile + 1) * share]


def compose_strip(blocks, earlier, plain, crossed, tiles, first):
    width = blocks.shape[1]
    slots = plain.shape[0]

    def kernel(*refs):
        strip_kernel(first, *refs)

    return pl.pallas_call(
        kernel,
        in_specs=[pl.BlockSpec(memory_space=pltpu.VMEM)] * 4,
        out_specs=pl.BlockSpec(memory_space=pltpu.VMEM),
        out_shape=pltpu.VMEM((tiles, 4, slots // tiles // 2, width), jnp.float32),
        name="strip",
    )(resident(blocks), resident(earlier), resident(plain), resident(crossed))


def stack_kernel(first, strips, out):
    slabs, _, share, _ = strips.shape
    totals = []
    for half in range(2):
        total = [strips[(slabs - 2 + half) ^ first, part] for part in range(4)]
        for slab in range(slabs - 4, -1, -2):
            front = [strips[(slab + half) ^ first, part] for part in range(4)]
            clear = 1.0 - front[3]
            total = [front[part] + clear * total[part] for part in range(4)]
        totals.append(total)
    for part in range(4):
        out[pl.ds(part, share, stride=4), :] = lefts(totals[0][part], totals[1][part])
        out[pl.ds(share * 4 + part, share, stride=4), :] = rights(totals[0][part], totals[1][part])


def stack(strips, first):
    _, _, share, width = strips.shape

    def kernel(*refs):
        stack_kernel(first, *refs)

    return pl.pallas_call(
        kernel,
        in_specs=[pl.BlockSpec(memory_space=pltpu.VMEM)],
        out_shape=jax.ShapeDtypeStruct((share * 8, width), jnp.float32),
        name="stack",
    )(resident(strips))


def shards(fragments, layer_rank, pixel_count, slot_count, block_run, brick_order, interlace):
    _, _, owners, capacity, _, width = fragments.shape
    slots = interlace.shape[0]
    tiles = lax.axis_size("depth")
    bricks = lax.axis_size("brick")
    first = tiles // 2 + 1
    root = (lax.axis_size("tile") // 2 + 1) * bricks + bricks // 2
    runs = np.split(np.arange(owners, dtype=np.int32), 2)[::-1]
    runs[0][[0, root - owners // 2]] = runs[0][[root - owners // 2, 0]]
    order = np.concatenate(runs)
    blocks = blend(fragments[0, 0], layer_rank[0, 0], pixel_count[0, 0].T, root)
    groups = [
        [int(owners * (2 * chip + core) + owner) for run in runs for core in (1, 0) for owner in run]
        for chip in range(tiles // 2)
    ]
    sent = lax.all_to_all(
        blocks.reshape(2 * owners, 4, width),
        ("depth", "tile", "brick"),
        split_axis=0,
        concat_axis=0,
        tiled=True,
        axis_index_groups=groups,
    )
    own = jnp.concatenate([slot_count[0], brick_order, block_run[0, 0].T], axis=0)
    other = lax.ppermute(own, "depth", [(place, place ^ 1) for place in range(tiles)])
    in_front = lax.axis_index("depth") % 2 == 0
    index = jnp.stack([jnp.where(in_front, own, other), jnp.where(in_front, other, own)])
    plans = plan(index, interlace.reshape(1, slots), jnp.asarray(order).reshape(1, owners), capacity, tiles)
    strip = compose_strip(sent.reshape(owners * 8, width), *plans, tiles, first)
    strips = lax.all_to_all(
        strip,
        "depth",
        split_axis=0,
        concat_axis=0,
        tiled=True,
        axis_index_groups=[[place ^ first for place in range(tiles)]],
    )
    return stack(strips, first).reshape(1, 1, slots // tiles, 4, width)


def solution(mesh):
    return jax.shard_map(
        shards,
        mesh=mesh,
        in_specs=(
            P("depth", ("tile", "brick"), None, None, None, None),
            P("depth", ("tile", "brick"), None, None, None),
            P("depth", ("tile", "brick"), None, None),
            P("depth", ("tile", "brick"), None),
            P("depth", ("tile", "brick"), None, None),
            P("depth", None),
            P(),
        ),
        out_specs=P(("tile", "brick"), "depth", None, None, None),
        check_vma=False,
    )
```

```python
import jax
import jax.numpy as jnp
import numpy as np
from jax import lax
from jax.experimental import pallas as pl
from jax.experimental.pallas import tpu as pltpu
from jax.sharding import PartitionSpec as P


def resident(array):
    return pltpu.with_memory_space_constraint(array, pltpu.VMEM)


def columns(row, rows, width):
    length = row.shape[1]
    place = lax.broadcasted_iota(jnp.int32, (rows, length), 1)
    own = lax.broadcasted_iota(jnp.int32, (rows, length), 0)
    spread = jnp.where(place == own, row.astype(jnp.float32), 0.0).astype(jnp.bfloat16)
    return jnp.dot(spread, jnp.ones((length, width), jnp.bfloat16), preferred_element_type=jnp.float32)


def reorder(row, order):
    length = row.shape[1]
    source = lax.broadcasted_iota(jnp.int32, (length, length), 0)
    chosen = jnp.where(source == order, 1.0, 0.0).astype(jnp.bfloat16)
    rows = jnp.broadcast_to(row.astype(jnp.float32), (8, length)).astype(jnp.bfloat16)
    return jnp.dot(rows, chosen, preferred_element_type=jnp.float32)[0:1, :].astype(jnp.int32)


def halves(values):
    high = values.astype(jnp.bfloat16)
    low = (values - high.astype(jnp.float32)).astype(jnp.bfloat16)
    return high, low


def picked(matrix, values):
    return jnp.dot(matrix, jnp.concatenate(halves(values), axis=0), preferred_element_type=jnp.float32)


def turned(values):
    return pltpu.roll(values, values.shape[-1] // 2, values.ndim - 1)


def in_left(values):
    lane = lax.broadcasted_iota(jnp.int32, values.shape, values.ndim - 1)
    return lane < values.shape[-1] // 2


def lefts(one, two):
    return jnp.where(in_left(one), one, turned(two))


def rights(one, two):
    return jnp.where(in_left(one), turned(one), two)


def blend_kernel(root, fragments, ranks, counts, out, pixels, layers, counted, mixed, *sems):
    capacity, owners = counts.shape
    width = out.shape[1]
    share = owners // 2
    pitch = pixels.shape[0] // owners
    wide = share * capacity * 4

    def fetched(step):
        rows = pl.ds(step * share, share)
        place = pixels.reshape(owners, pitch, width).at[rows, pl.ds(0, capacity * 16)]
        return pltpu.make_async_copy(fragments.at[rows], place, sems[0].at[step])

    def stored(step):
        rows = pl.ds((1 - step) * wide, wide)
        return pltpu.make_async_copy(mixed.at[rows], out.at[rows], sems[1].at[step])

    rank_copy = pltpu.make_async_copy(ranks, layers, sems[2])
    count_copy = pltpu.make_async_copy(counts, counted, sems[3])
    fetched(1).start()
    rank_copy.start()
    count_copy.start()
    fetched(0).start()
    pixel = lax.broadcasted_iota(jnp.int32, (owners, width), 1).astype(jnp.float32)
    visible = None
    for step in (1, 0):
        if visible is None:
            rank_copy.wait()
            count_copy.wait()
            visible = [
                jnp.where(pixel < columns(counted[slot : slot + 1, :], owners, width), 1.0, 0.0)
                for slot in range(capacity)
            ]
        fetched(step).wait()
        blended = []
        for slot in range(capacity):
            rank = [
                layers[pl.ds(step * wide + slot * 4 + layer, share, stride=capacity * 4), :] for layer in range(4)
            ]
            entry = [
                [
                    pixels[pl.ds(step * share * pitch + slot * 16 + layer * 4 + part, share, stride=pitch), :]
                    for part in range(4)
                ]
                for layer in range(4)
            ]
            clear = [1.0 - entry[layer][3] for layer in range(4)]
            weight = [visible[slot][step * share : (step + 1) * share]] * 4
            for one in range(4):
                for two in range(one + 1, 4):
                    ahead = rank[one] < rank[two]
                    weight[two] = weight[two] * jnp.where(ahead, clear[one], 1.0)
                    weight[one] = weight[one] * jnp.where(ahead, 1.0, clear[two])
            blended.append([])
            for part in range(4):
                total = entry[0][part] * weight[0]
                for layer in range(1, 4):
                    total = total + entry[layer][part] * weight[layer]
                blended[slot].append(total)
        base = (1 - step) * wide
        for part in range(4):
            one, two = blended[0][part], blended[1][part]
            mixed[pl.ds(base + part, share, stride=4), :] = rights(one, two)
            mixed[pl.ds(base + wide // 2 + part, share, stride=4), :] = lefts(one, two)
        if step == 1:
            for half in range(2):
                first = pl.ds(half * wide // 2, 4)
                other = pl.ds(half * wide // 2 + (root - share) * 4, 4)
                moved = mixed[first, :]
                mixed[first, :] = mixed[other, :]
                mixed[other, :] = moved
        stored(step).start()
    for step in (1, 0):
        stored(step).wait()


def blend(fragments, ranks, counts, root):
    owners, capacity, _, width = fragments.shape
    rows = owners * capacity

    def kernel(*refs):
        blend_kernel(root, *refs)

    return pl.pallas_call(
        kernel,
        in_specs=[pl.BlockSpec(memory_space=pl.ANY)] * 3,
        out_specs=pl.BlockSpec(memory_space=pl.ANY),
        out_shape=jax.ShapeDtypeStruct((rows * 4, width), jnp.float32),
        scratch_shapes=[
            pltpu.VMEM((owners * (capacity * 16 + 8), width), jnp.float32),
            pltpu.VMEM((rows * 4, width), jnp.int32),
            pltpu.VMEM((capacity, owners), jnp.int32),
            pltpu.VMEM((rows * 4, width), jnp.float32),
            pltpu.SemaphoreType.DMA((2,)),
            pltpu.SemaphoreType.DMA((2,)),
            pltpu.SemaphoreType.DMA,
            pltpu.SemaphoreType.DMA,
        ],
        name="blend",
    )(fragments.reshape(owners, capacity * 16, width), ranks.reshape(rows * 4, width), counts)


def plan_kernel(capacity, tiles, index, interlace, placed, earlier, plain, crossed):
    bricks = placed.shape[1]
    slots = interlace.shape[1]
    total = capacity * bricks
    place = placed[...]
    gap = slots // tiles // 2
    row = lax.broadcasted_iota(jnp.int32, (slots // 2, total), 0)
    near = row + row // gap * gap

    def store(target, slab, chosen):
        ones = jnp.where(chosen, 1.0, 0.0).astype(jnp.bfloat16)
        rows = ones.shape[0]
        target[slab * rows : (slab + 1) * rows, :] = jnp.concatenate([ones, ones], axis=1)

    for slab in range(2):
        count = reorder(index[slab, 0:1, :], place)
        rank = jnp.concatenate([reorder(index[slab, 1:2, :], place)] * capacity, axis=1)
        run = jnp.concatenate(
            [reorder(index[slab, 2 + slot : 3 + slot, :], place) for slot in range(capacity)], axis=1
        )
        live = jnp.concatenate([jnp.where(count > slot, 1, 0) for slot in range(capacity)], axis=1) > 0
        run_of = columns(run, total, total).astype(jnp.int32)
        rank_of = columns(rank, total, total).astype(jnp.int32)
        store(earlier, slab, (run_of == run) & (rank < rank_of) & live)
        slot_id = lax.broadcasted_iota(jnp.int32, (slots, total), 0)
        landing = jnp.where(slot_id == run, 1.0, 0.0).astype(jnp.bfloat16)
        screen = jnp.dot(
            jnp.broadcast_to(interlace[...].astype(jnp.float32), (8, slots)).astype(jnp.bfloat16),
            landing,
            preferred_element_type=jnp.float32,
        )[0:1, :].astype(jnp.int32)
        store((plain, crossed)[slab], slab, (near == screen) & live)
        store((crossed, plain)[slab], slab, (near + gap == screen) & live)


def plan(index, interlace, placed, capacity, tiles):
    total = capacity * placed.shape[1]
    slots = interlace.shape[1]

    def kernel(*refs):
        plan_kernel(capacity, tiles, *refs)

    return pl.pallas_call(
        kernel,
        out_specs=(pl.BlockSpec(memory_space=pltpu.VMEM),) * 3,
        out_shape=(
            pltpu.VMEM((2 * total, 2 * total), jnp.bfloat16),
            pltpu.VMEM((slots, 2 * total), jnp.bfloat16),
            pltpu.VMEM((slots, 2 * total), jnp.bfloat16),
        ),
        name="plan",
    )(index, interlace, placed)


def strip_kernel(first, blocks, earlier, plain, crossed, out):
    tiles, _, share, width = out.shape
    quarter = blocks.shape[0] // 4

    def rows_of(side, part):
        return jnp.concatenate(
            [blocks[pl.ds((2 * run + side) * quarter + part, quarter // 4, stride=4), :] for run in range(2)], axis=0
        )

    def part_of(part):
        front, back = rows_of(1, part), rows_of(0, part)
        left, front_turned, back_turned = in_left(front), turned(front), turned(back)
        plain_rows = [jnp.where(left, front, back_turned), jnp.where(left, front_turned, back)]
        crossed_rows = [jnp.where(left, back, front_turned), jnp.where(left, back_turned, front)]
        return jnp.concatenate(plain_rows, axis=0), jnp.concatenate(crossed_rows, axis=0)

    def sides(values):
        half = values.shape[0] // 2
        return values[:half], values[half:]

    parts = [part_of(part) for part in range(4)]
    front, back = sides(picked(earlier[...], jnp.log(1.0 - parts[3][0])))
    passed = jnp.exp(jnp.where(in_left(front), front, back))
    here = jnp.concatenate([part[0] * passed for part in parts], axis=1)
    here_front, here_back = sides(picked(plain[...], here))
    passed = turned(passed)
    there = jnp.concatenate([part[1] * passed for part in parts], axis=1)
    there_front, there_back = sides(picked(crossed[...], there))
    fronts, backs = [], []
    for part in range(4):
        lanes = slice(part * width, (part + 1) * width)
        left = in_left(here_front[:, lanes])
        fronts.append(jnp.where(left, here_front[:, lanes], there_front[:, lanes]))
        backs.append(jnp.where(left, there_back[:, lanes], here_back[:, lanes]))
    clear = 1.0 - fronts[3]
    for part in range(4):
        merged = fronts[part] + clear * backs[part]
        for tile in range(tiles):
            out[tile ^ first, part] = merged[tile * share : (tile + 1) * share]


def compose_strip(blocks, earlier, plain, crossed, tiles, first):
    width = blocks.shape[1]
    slots = plain.shape[0]

    def kernel(*refs):
        strip_kernel(first, *refs)

    return pl.pallas_call(
        kernel,
        in_specs=[pl.BlockSpec(memory_space=pltpu.VMEM)] * 4,
        out_specs=pl.BlockSpec(memory_space=pltpu.VMEM),
        out_shape=pltpu.VMEM((tiles, 4, slots // tiles // 2, width), jnp.float32),
        name="strip",
    )(resident(blocks), resident(earlier), resident(plain), resident(crossed))


def stack_kernel(first, strips, out):
    slabs, _, share, _ = strips.shape
    totals = []
    for half in range(2):
        total = [strips[(slabs - 2 + half) ^ first, part] for part in range(4)]
        for slab in range(slabs - 4, -1, -2):
            front = [strips[(slab + half) ^ first, part] for part in range(4)]
            clear = 1.0 - front[3]
            total = [front[part] + clear * total[part] for part in range(4)]
        totals.append(total)
    for part in range(4):
        out[pl.ds(part, share, stride=4), :] = lefts(totals[0][part], totals[1][part])
        out[pl.ds(share * 4 + part, share, stride=4), :] = rights(totals[0][part], totals[1][part])


def stack(strips, first):
    _, _, share, width = strips.shape

    def kernel(*refs):
        stack_kernel(first, *refs)

    return pl.pallas_call(
        kernel,
        in_specs=[pl.BlockSpec(memory_space=pltpu.VMEM)],
        out_shape=jax.ShapeDtypeStruct((share * 8, width), jnp.float32),
        name="stack",
    )(resident(strips))


def shards(fragments, layer_rank, pixel_count, slot_count, block_run, brick_order, interlace):
    _, _, owners, capacity, _, width = fragments.shape
    slots = interlace.shape[0]
    tiles = lax.axis_size("depth")
    bricks = lax.axis_size("brick")
    first = tiles // 2 + 1
    root = (lax.axis_size("tile") // 2 + 1) * bricks + bricks // 2
    runs = np.split(np.arange(owners, dtype=np.int32), 2)[::-1]
    runs[0][[0, root - owners // 2]] = runs[0][[root - owners // 2, 0]]
    order = np.concatenate(runs)
    blocks = blend(fragments[0, 0], layer_rank[0, 0], pixel_count[0, 0].T, root)
    groups = [
        [int(owners * (2 * chip + core) + owner) for run in runs for core in (1, 0) for owner in run]
        for chip in range(tiles // 2)
    ]
    sent = lax.all_to_all(
        blocks.reshape(2 * owners, 4, width),
        ("depth", "tile", "brick"),
        split_axis=0,
        concat_axis=0,
        tiled=True,
        axis_index_groups=groups,
    )
    own = jnp.concatenate([slot_count[0], brick_order, block_run[0, 0].T], axis=0)
    other = lax.ppermute(own, "depth", [(place, place ^ 1) for place in range(tiles)])
    in_front = lax.axis_index("depth") % 2 == 0
    index = jnp.stack([jnp.where(in_front, own, other), jnp.where(in_front, other, own)])
    plans = plan(index, interlace.reshape(1, slots), jnp.asarray(order).reshape(1, owners), capacity, tiles)
    strip = compose_strip(sent.reshape(owners * 8, width), *plans, tiles, first)
    strips = lax.all_to_all(
        strip,
        "depth",
        split_axis=0,
        concat_axis=0,
        tiled=True,
        axis_index_groups=[[place ^ first for place in range(tiles)]],
    )
    return stack(strips, first).reshape(1, 1, slots // tiles, 4, width)


def solution(mesh):
    return jax.shard_map(
        shards,
        mesh=mesh,
        in_specs=(
            P("depth", ("tile", "brick"), None, None, None, None),
            P("depth", ("tile", "brick"), None, None, None),
            P("depth", ("tile", "brick"), None, None),
            P("depth", ("tile", "brick"), None),
            P("depth", ("tile", "brick"), None, None),
            P("depth", None),
            P(),
        ),
        out_specs=P(("tile", "brick"), "depth", None, None, None),
        check_vma=False,
    )
```

```python
import jax
import jax.numpy as jnp
import numpy as np
from jax import lax
from jax.experimental import pallas as pl
from jax.experimental.pallas import tpu as pltpu
from jax.sharding import PartitionSpec as P


def resident(array):
    return pltpu.with_memory_space_constraint(array, pltpu.VMEM)


def columns(row, rows, width):
    length = row.shape[1]
    place = lax.broadcasted_iota(jnp.int32, (rows, length), 1)
    own = lax.broadcasted_iota(jnp.int32, (rows, length), 0)
    spread = jnp.where(place == own, row.astype(jnp.float32), 0.0).astype(jnp.bfloat16)
    return jnp.dot(spread, jnp.ones((length, width), jnp.bfloat16), preferred_element_type=jnp.float32)


def reorder(row, order):
    length = row.shape[1]
    source = lax.broadcasted_iota(jnp.int32, (length, length), 0)
    chosen = jnp.where(source == order, 1.0, 0.0).astype(jnp.bfloat16)
    rows = jnp.broadcast_to(row.astype(jnp.float32), (8, length)).astype(jnp.bfloat16)
    return jnp.dot(rows, chosen, preferred_element_type=jnp.float32)[0:1, :].astype(jnp.int32)


def halves(values):
    high = values.astype(jnp.bfloat16)
    low = (values - high.astype(jnp.float32)).astype(jnp.bfloat16)
    return high, low


def picked(matrix, values):
    return jnp.dot(matrix, jnp.concatenate(halves(values), axis=0), preferred_element_type=jnp.float32)


def turned(values):
    return pltpu.roll(values, values.shape[-1] // 2, values.ndim - 1)


def in_left(values):
    lane = lax.broadcasted_iota(jnp.int32, values.shape, values.ndim - 1)
    return lane < values.shape[-1] // 2


def lefts(one, two):
    return jnp.where(in_left(one), one, turned(two))


def rights(one, two):
    return jnp.where(in_left(one), turned(one), two)


def blend_kernel(root, fragments, ranks, counts, out, pixels, layers, counted, mixed, *sems):
    capacity, owners = counts.shape
    width = out.shape[1]
    share = owners // 2
    pitch = pixels.shape[0] // owners
    wide = share * capacity * 4

    def fetched(step):
        rows = pl.ds(step * share, share)
        place = pixels.reshape(owners, pitch, width).at[rows, pl.ds(0, capacity * 16)]
        return pltpu.make_async_copy(fragments.at[rows], place, sems[0].at[step])

    def stored(step):
        rows = pl.ds((1 - step) * wide, wide)
        return pltpu.make_async_copy(mixed.at[rows], out.at[rows], sems[1].at[step])

    rank_copy = pltpu.make_async_copy(ranks, layers, sems[2])
    count_copy = pltpu.make_async_copy(counts, counted, sems[3])
    fetched(1).start()
    rank_copy.start()
    count_copy.start()
    fetched(0).start()
    pixel = lax.broadcasted_iota(jnp.int32, (owners, width), 1).astype(jnp.float32)
    visible = None
    for step in (1, 0):
        if visible is None:
            rank_copy.wait()
            count_copy.wait()
            visible = [
                jnp.where(pixel < columns(counted[slot : slot + 1, :], owners, width), 1.0, 0.0)
                for slot in range(capacity)
            ]
        fetched(step).wait()
        blended = []
        for slot in range(capacity):
            rank = [
                layers[pl.ds(step * wide + slot * 4 + layer, share, stride=capacity * 4), :] for layer in range(4)
            ]
            entry = [
                [
                    pixels[pl.ds(step * share * pitch + slot * 16 + layer * 4 + part, share, stride=pitch), :]
                    for part in range(4)
                ]
                for layer in range(4)
            ]
            clear = [1.0 - entry[layer][3] for layer in range(4)]
            weight = [visible[slot][step * share : (step + 1) * share]] * 4
            for one in range(4):
                for two in range(one + 1, 4):
                    ahead = rank[one] < rank[two]
                    weight[two] = weight[two] * jnp.where(ahead, clear[one], 1.0)
                    weight[one] = weight[one] * jnp.where(ahead, 1.0, clear[two])
            blended.append([])
            for part in range(4):
                total = entry[0][part] * weight[0]
                for layer in range(1, 4):
                    total = total + entry[layer][part] * weight[layer]
                blended[slot].append(total)
        base = (1 - step) * wide
        for part in range(4):
            one, two = blended[0][part], blended[1][part]
            mixed[pl.ds(base + part, share, stride=4), :] = rights(one, two)
            mixed[pl.ds(base + wide // 2 + part, share, stride=4), :] = lefts(one, two)
        if step == 1:
            for half in range(2):
                first = pl.ds(half * wide // 2, 4)
                other = pl.ds(half * wide // 2 + (root - share) * 4, 4)
                moved = mixed[first, :]
                mixed[first, :] = mixed[other, :]
                mixed[other, :] = moved
        stored(step).start()
    for step in (1, 0):
        stored(step).wait()


def blend(fragments, ranks, counts, root):
    owners, capacity, _, width = fragments.shape
    rows = owners * capacity

    def kernel(*refs):
        blend_kernel(root, *refs)

    return pl.pallas_call(
        kernel,
        in_specs=[pl.BlockSpec(memory_space=pl.ANY)] * 3,
        out_specs=pl.BlockSpec(memory_space=pl.ANY),
        out_shape=jax.ShapeDtypeStruct((rows * 4, width), jnp.float32),
        scratch_shapes=[
            pltpu.VMEM((owners * (capacity * 16 + 8), width), jnp.float32),
            pltpu.VMEM((rows * 4, width), jnp.int32),
            pltpu.VMEM((capacity, owners), jnp.int32),
            pltpu.VMEM((rows * 4, width), jnp.float32),
            pltpu.SemaphoreType.DMA((2,)),
            pltpu.SemaphoreType.DMA((2,)),
            pltpu.SemaphoreType.DMA,
            pltpu.SemaphoreType.DMA,
        ],
        name="blend",
    )(fragments.reshape(owners, capacity * 16, width), ranks.reshape(rows * 4, width), counts)


def plan_kernel(capacity, tiles, index, interlace, placed, earlier, plain, crossed):
    bricks = placed.shape[1]
    slots = interlace.shape[1]
    total = capacity * bricks
    place = placed[...]
    gap = slots // tiles // 2
    row = lax.broadcasted_iota(jnp.int32, (slots // 2, total), 0)
    near = row + row // gap * gap

    def store(target, slab, chosen):
        ones = jnp.where(chosen, 1.0, 0.0).astype(jnp.bfloat16)
        rows = ones.shape[0]
        target[slab * rows : (slab + 1) * rows, :] = jnp.concatenate([ones, ones], axis=1)

    for slab in range(2):
        count = reorder(index[slab, 0:1, :], place)
        rank = jnp.concatenate([reorder(index[slab, 1:2, :], place)] * capacity, axis=1)
        run = jnp.concatenate(
            [reorder(index[slab, 2 + slot : 3 + slot, :], place) for slot in range(capacity)], axis=1
        )
        live = jnp.concatenate([jnp.where(count > slot, 1, 0) for slot in range(capacity)], axis=1) > 0
        run_of = columns(run, total, total).astype(jnp.int32)
        rank_of = columns(rank, total, total).astype(jnp.int32)
        store(earlier, slab, (run_of == run) & (rank < rank_of) & live)
        slot_id = lax.broadcasted_iota(jnp.int32, (slots, total), 0)
        landing = jnp.where(slot_id == run, 1.0, 0.0).astype(jnp.bfloat16)
        screen = jnp.dot(
            jnp.broadcast_to(interlace[...].astype(jnp.float32), (8, slots)).astype(jnp.bfloat16),
            landing,
            preferred_element_type=jnp.float32,
        )[0:1, :].astype(jnp.int32)
        store((plain, crossed)[slab], slab, (near == screen) & live)
        store((crossed, plain)[slab], slab, (near + gap == screen) & live)


def plan(index, interlace, placed, capacity, tiles):
    total = capacity * placed.shape[1]
    slots = interlace.shape[1]

    def kernel(*refs):
        plan_kernel(capacity, tiles, *refs)

    return pl.pallas_call(
        kernel,
        out_specs=(pl.BlockSpec(memory_space=pltpu.VMEM),) * 3,
        out_shape=(
            pltpu.VMEM((2 * total, 2 * total), jnp.bfloat16),
            pltpu.VMEM((slots, 2 * total), jnp.bfloat16),
            pltpu.VMEM((slots, 2 * total), jnp.bfloat16),
        ),
        name="plan",
    )(index, interlace, placed)


def strip_kernel(first, blocks, earlier, plain, crossed, out):
    tiles, _, share, width = out.shape
    quarter = blocks.shape[0] // 4

    def rows_of(side, part):
        return jnp.concatenate(
            [blocks[pl.ds((2 * run + side) * quarter + part, quarter // 4, stride=4), :] for run in range(2)], axis=0
        )

    def part_of(part):
        front, back = rows_of(1, part), rows_of(0, part)
        left, front_turned, back_turned = in_left(front), turned(front), turned(back)
        plain_rows = [jnp.where(left, front, back_turned), jnp.where(left, front_turned, back)]
        crossed_rows = [jnp.where(left, back, front_turned), jnp.where(left, back_turned, front)]
        return jnp.concatenate(plain_rows, axis=0), jnp.concatenate(crossed_rows, axis=0)

    def sides(values):
        half = values.shape[0] // 2
        return values[:half], values[half:]

    parts = [part_of(part) for part in range(4)]
    front, back = sides(picked(earlier[...], jnp.log(1.0 - parts[3][0])))
    passed = jnp.exp(jnp.where(in_left(front), front, back))
    here = jnp.concatenate([part[0] * passed for part in parts], axis=1)
    here_front, here_back = sides(picked(plain[...], here))
    passed = turned(passed)
    there = jnp.concatenate([part[1] * passed for part in parts], axis=1)
    there_front, there_back = sides(picked(crossed[...], there))
    fronts, backs = [], []
    for part in range(4):
        lanes = slice(part * width, (part + 1) * width)
        left = in_left(here_front[:, lanes])
        fronts.append(jnp.where(left, here_front[:, lanes], there_front[:, lanes]))
        backs.append(jnp.where(left, there_back[:, lanes], here_back[:, lanes]))
    clear = 1.0 - fronts[3]
    for part in range(4):
        merged = fronts[part] + clear * backs[part]
        for tile in range(tiles):
            out[first.index(tile), part] = merged[tile * share : (tile + 1) * share]


def compose_strip(blocks, earlier, plain, crossed, tiles, first):
    width = blocks.shape[1]
    slots = plain.shape[0]

    def kernel(*refs):
        strip_kernel(first, *refs)

    return pl.pallas_call(
        kernel,
        in_specs=[pl.BlockSpec(memory_space=pltpu.VMEM)] * 4,
        out_specs=pl.BlockSpec(memory_space=pltpu.VMEM),
        out_shape=pltpu.VMEM((tiles, 4, slots // tiles // 2, width), jnp.float32),
        name="strip",
    )(resident(blocks), resident(earlier), resident(plain), resident(crossed))


def stack_kernel(first, strips, out):
    slabs, _, share, _ = strips.shape
    totals = []
    for half in range(2):
        total = [strips[first.index(slabs - 2 + half), part] for part in range(4)]
        for slab in range(slabs - 4, -1, -2):
            front = [strips[first.index(slab + half), part] for part in range(4)]
            clear = 1.0 - front[3]
            total = [front[part] + clear * total[part] for part in range(4)]
        totals.append(total)
    for part in range(4):
        out[pl.ds(part, share, stride=4), :] = lefts(totals[0][part], totals[1][part])
        out[pl.ds(share * 4 + part, share, stride=4), :] = rights(totals[0][part], totals[1][part])


def stack(strips, first):
    _, _, share, width = strips.shape

    def kernel(*refs):
        stack_kernel(first, *refs)

    return pl.pallas_call(
        kernel,
        in_specs=[pl.BlockSpec(memory_space=pltpu.VMEM)],
        out_shape=jax.ShapeDtypeStruct((share * 8, width), jnp.float32),
        name="stack",
    )(resident(strips))


def shards(fragments, layer_rank, pixel_count, slot_count, block_run, brick_order, interlace):
    _, _, owners, capacity, _, width = fragments.shape
    slots = interlace.shape[0]
    tiles = lax.axis_size("depth")
    bricks = lax.axis_size("brick")
    middle = tiles // 2
    first = [middle + 1, middle, *range(middle + 2, tiles), *range(middle - 2, middle), *range(middle - 2)]
    root = (lax.axis_size("tile") // 2 + 1) * bricks + bricks // 2
    runs = np.split(np.arange(owners, dtype=np.int32), 2)[::-1]
    runs[0][[0, root - owners // 2]] = runs[0][[root - owners // 2, 0]]
    order = np.concatenate(runs)
    blocks = blend(fragments[0, 0], layer_rank[0, 0], pixel_count[0, 0].T, root)
    groups = [
        [int(owners * (2 * chip + core) + owner) for run in runs for core in (1, 0) for owner in run]
        for chip in range(tiles // 2)
    ]
    sent = lax.all_to_all(
        blocks.reshape(2 * owners, 4, width),
        ("depth", "tile", "brick"),
        split_axis=0,
        concat_axis=0,
        tiled=True,
        axis_index_groups=groups,
    )
    own = jnp.concatenate([slot_count[0], brick_order, block_run[0, 0].T], axis=0)
    other = lax.ppermute(own, "depth", [(place, place ^ 1) for place in range(tiles)])
    in_front = lax.axis_index("depth") % 2 == 0
    index = jnp.stack([jnp.where(in_front, own, other), jnp.where(in_front, other, own)])
    plans = plan(index, interlace.reshape(1, slots), jnp.asarray(order).reshape(1, owners), capacity, tiles)
    strip = compose_strip(sent.reshape(owners * 8, width), *plans, tiles, first)
    strips = lax.all_to_all(
        strip,
        "depth",
        split_axis=0,
        concat_axis=0,
        tiled=True,
        axis_index_groups=[first],
    )
    return stack(strips, first).reshape(1, 1, slots // tiles, 4, width)


def solution(mesh):
    return jax.shard_map(
        shards,
        mesh=mesh,
        in_specs=(
            P("depth", ("tile", "brick"), None, None, None, None),
            P("depth", ("tile", "brick"), None, None, None),
            P("depth", ("tile", "brick"), None, None),
            P("depth", ("tile", "brick"), None),
            P("depth", ("tile", "brick"), None, None),
            P("depth", None),
            P(),
        ),
        out_specs=P(("tile", "brick"), "depth", None, None, None),
        check_vma=False,
    )
```

```python
import jax
import jax.numpy as jnp
import numpy as np
from jax import lax
from jax.experimental import pallas as pl
from jax.experimental.pallas import tpu as pltpu
from jax.sharding import PartitionSpec as P


def resident(array):
    return pltpu.with_memory_space_constraint(array, pltpu.VMEM)


def columns(row, rows, width):
    length = row.shape[1]
    place = lax.broadcasted_iota(jnp.int32, (rows, length), 1)
    own = lax.broadcasted_iota(jnp.int32, (rows, length), 0)
    spread = jnp.where(place == own, row.astype(jnp.float32), 0.0).astype(jnp.bfloat16)
    return jnp.dot(spread, jnp.ones((length, width), jnp.bfloat16), preferred_element_type=jnp.float32)


def reorder(row, order):
    length = row.shape[1]
    source = lax.broadcasted_iota(jnp.int32, (length, length), 0)
    chosen = jnp.where(source == order, 1.0, 0.0).astype(jnp.bfloat16)
    rows = jnp.broadcast_to(row.astype(jnp.float32), (8, length)).astype(jnp.bfloat16)
    return jnp.dot(rows, chosen, preferred_element_type=jnp.float32)[0:1, :].astype(jnp.int32)


def halves(values):
    high = values.astype(jnp.bfloat16)
    low = (values - high.astype(jnp.float32)).astype(jnp.bfloat16)
    return high, low


def picked(matrix, values):
    return jnp.dot(matrix, jnp.concatenate(halves(values), axis=0), preferred_element_type=jnp.float32)


def turned(values):
    return pltpu.roll(values, values.shape[-1] // 2, values.ndim - 1)


def in_left(values):
    lane = lax.broadcasted_iota(jnp.int32, values.shape, values.ndim - 1)
    return lane < values.shape[-1] // 2


def lefts(one, two):
    return jnp.where(in_left(one), one, turned(two))


def rights(one, two):
    return jnp.where(in_left(one), turned(one), two)


def blend_kernel(root, fragments, ranks, counts, out, pixels, layers, counted, mixed, *sems):
    capacity, owners = counts.shape
    width = out.shape[1]
    share = owners // 2
    pitch = pixels.shape[0] // owners
    wide = share * capacity * 4

    def fetched(step):
        rows = pl.ds(step * share, share)
        place = pixels.reshape(owners, pitch, width).at[rows, pl.ds(0, capacity * 16)]
        return pltpu.make_async_copy(fragments.at[rows], place, sems[0].at[step])

    def stored(step):
        rows = pl.ds((1 - step) * wide, wide)
        return pltpu.make_async_copy(mixed.at[rows], out.at[rows], sems[1].at[step])

    rank_copy = pltpu.make_async_copy(ranks, layers, sems[2])
    count_copy = pltpu.make_async_copy(counts, counted, sems[3])
    rank_copy.start()
    fetched(1).start()
    fetched(0).start()
    count_copy.start()
    pixel = lax.broadcasted_iota(jnp.int32, (owners, width), 1).astype(jnp.float32)
    visible = None
    for step in (1, 0):
        if visible is None:
            rank_copy.wait()
            count_copy.wait()
            visible = [
                jnp.where(pixel < columns(counted[slot : slot + 1, :], owners, width), 1.0, 0.0)
                for slot in range(capacity)
            ]
        fetched(step).wait()
        blended = []
        for slot in range(capacity):
            rank = [
                layers[pl.ds(step * wide + slot * 4 + layer, share, stride=capacity * 4), :] for layer in range(4)
            ]
            entry = [
                [
                    pixels[pl.ds(step * share * pitch + slot * 16 + layer * 4 + part, share, stride=pitch), :]
                    for part in range(4)
                ]
                for layer in range(4)
            ]
            clear = [1.0 - entry[layer][3] for layer in range(4)]
            weight = [visible[slot][step * share : (step + 1) * share]] * 4
            for one in range(4):
                for two in range(one + 1, 4):
                    ahead = rank[one] < rank[two]
                    weight[two] = weight[two] * jnp.where(ahead, clear[one], 1.0)
                    weight[one] = weight[one] * jnp.where(ahead, 1.0, clear[two])
            blended.append([])
            for part in range(4):
                total = entry[0][part] * weight[0]
                for layer in range(1, 4):
                    total = total + entry[layer][part] * weight[layer]
                blended[slot].append(total)
        base = (1 - step) * wide
        for part in range(4):
            one, two = blended[0][part], blended[1][part]
            mixed[pl.ds(base + part, share, stride=4), :] = rights(one, two)
            mixed[pl.ds(base + wide // 2 + part, share, stride=4), :] = lefts(one, two)
        if step == 1:
            for half in range(2):
                first = pl.ds(half * wide // 2, 4)
                other = pl.ds(half * wide // 2 + (root - share) * 4, 4)
                moved = mixed[first, :]
                mixed[first, :] = mixed[other, :]
                mixed[other, :] = moved
        stored(step).start()
    for step in (1, 0):
        stored(step).wait()


def blend(fragments, ranks, counts, root):
    owners, capacity, _, width = fragments.shape
    rows = owners * capacity

    def kernel(*refs):
        blend_kernel(root, *refs)

    return pl.pallas_call(
        kernel,
        in_specs=[pl.BlockSpec(memory_space=pl.ANY)] * 3,
        out_specs=pl.BlockSpec(memory_space=pl.ANY),
        out_shape=jax.ShapeDtypeStruct((rows * 4, width), jnp.float32),
        scratch_shapes=[
            pltpu.VMEM((owners * (capacity * 16 + 8), width), jnp.float32),
            pltpu.VMEM((rows * 4, width), jnp.int32),
            pltpu.VMEM((capacity, owners), jnp.int32),
            pltpu.VMEM((rows * 4, width), jnp.float32),
            pltpu.SemaphoreType.DMA((2,)),
            pltpu.SemaphoreType.DMA((2,)),
            pltpu.SemaphoreType.DMA,
            pltpu.SemaphoreType.DMA,
        ],
        name="blend",
    )(fragments.reshape(owners, capacity * 16, width), ranks.reshape(rows * 4, width), counts)


def plan_kernel(capacity, tiles, index, interlace, placed, earlier, plain, crossed):
    bricks = placed.shape[1]
    slots = interlace.shape[1]
    total = capacity * bricks
    place = placed[...]
    gap = slots // tiles // 2
    row = lax.broadcasted_iota(jnp.int32, (slots // 2, total), 0)
    near = row + row // gap * gap

    def store(target, slab, chosen):
        ones = jnp.where(chosen, 1.0, 0.0).astype(jnp.bfloat16)
        rows = ones.shape[0]
        target[slab * rows : (slab + 1) * rows, :] = jnp.concatenate([ones, ones], axis=1)

    for slab in range(2):
        count = reorder(index[slab, 0:1, :], place)
        rank = jnp.concatenate([reorder(index[slab, 1:2, :], place)] * capacity, axis=1)
        run = jnp.concatenate(
            [reorder(index[slab, 2 + slot : 3 + slot, :], place) for slot in range(capacity)], axis=1
        )
        live = jnp.concatenate([jnp.where(count > slot, 1, 0) for slot in range(capacity)], axis=1) > 0
        run_of = columns(run, total, total).astype(jnp.int32)
        rank_of = columns(rank, total, total).astype(jnp.int32)
        store(earlier, slab, (run_of == run) & (rank < rank_of) & live)
        slot_id = lax.broadcasted_iota(jnp.int32, (slots, total), 0)
        landing = jnp.where(slot_id == run, 1.0, 0.0).astype(jnp.bfloat16)
        screen = jnp.dot(
            jnp.broadcast_to(interlace[...].astype(jnp.float32), (8, slots)).astype(jnp.bfloat16),
            landing,
            preferred_element_type=jnp.float32,
        )[0:1, :].astype(jnp.int32)
        store((plain, crossed)[slab], slab, (near == screen) & live)
        store((crossed, plain)[slab], slab, (near + gap == screen) & live)


def plan(index, interlace, placed, capacity, tiles):
    total = capacity * placed.shape[1]
    slots = interlace.shape[1]

    def kernel(*refs):
        plan_kernel(capacity, tiles, *refs)

    return pl.pallas_call(
        kernel,
        out_specs=(pl.BlockSpec(memory_space=pltpu.VMEM),) * 3,
        out_shape=(
            pltpu.VMEM((2 * total, 2 * total), jnp.bfloat16),
            pltpu.VMEM((slots, 2 * total), jnp.bfloat16),
            pltpu.VMEM((slots, 2 * total), jnp.bfloat16),
        ),
        name="plan",
    )(index, interlace, placed)


def strip_kernel(first, blocks, earlier, plain, crossed, out):
    tiles, _, share, width = out.shape
    quarter = blocks.shape[0] // 4

    def rows_of(side, part):
        return jnp.concatenate(
            [blocks[pl.ds((2 * run + side) * quarter + part, quarter // 4, stride=4), :] for run in range(2)], axis=0
        )

    def part_of(part):
        front, back = rows_of(1, part), rows_of(0, part)
        left, front_turned, back_turned = in_left(front), turned(front), turned(back)
        plain_rows = [jnp.where(left, front, back_turned), jnp.where(left, front_turned, back)]
        crossed_rows = [jnp.where(left, back, front_turned), jnp.where(left, back_turned, front)]
        return jnp.concatenate(plain_rows, axis=0), jnp.concatenate(crossed_rows, axis=0)

    def sides(values):
        half = values.shape[0] // 2
        return values[:half], values[half:]

    parts = [part_of(part) for part in range(4)]
    front, back = sides(picked(earlier[...], jnp.log(1.0 - parts[3][0])))
    passed = jnp.exp(jnp.where(in_left(front), front, back))
    here = jnp.concatenate([part[0] * passed for part in parts], axis=1)
    here_front, here_back = sides(picked(plain[...], here))
    passed = turned(passed)
    there = jnp.concatenate([part[1] * passed for part in parts], axis=1)
    there_front, there_back = sides(picked(crossed[...], there))
    fronts, backs = [], []
    for part in range(4):
        lanes = slice(part * width, (part + 1) * width)
        left = in_left(here_front[:, lanes])
        fronts.append(jnp.where(left, here_front[:, lanes], there_front[:, lanes]))
        backs.append(jnp.where(left, there_back[:, lanes], here_back[:, lanes]))
    clear = 1.0 - fronts[3]
    for part in range(4):
        merged = fronts[part] + clear * backs[part]
        for tile in range(tiles):
            out[first.index(tile), part] = merged[tile * share : (tile + 1) * share]


def compose_strip(blocks, earlier, plain, crossed, tiles, first):
    width = blocks.shape[1]
    slots = plain.shape[0]

    def kernel(*refs):
        strip_kernel(first, *refs)

    return pl.pallas_call(
        kernel,
        in_specs=[pl.BlockSpec(memory_space=pltpu.VMEM)] * 4,
        out_specs=pl.BlockSpec(memory_space=pltpu.VMEM),
        out_shape=pltpu.VMEM((tiles, 4, slots // tiles // 2, width), jnp.float32),
        name="strip",
    )(resident(blocks), resident(earlier), resident(plain), resident(crossed))


def stack_kernel(first, strips, out):
    slabs, _, share, _ = strips.shape
    totals = []
    for half in range(2):
        total = [strips[first.index(slabs - 2 + half), part] for part in range(4)]
        for slab in range(slabs - 4, -1, -2):
            front = [strips[first.index(slab + half), part] for part in range(4)]
            clear = 1.0 - front[3]
            total = [front[part] + clear * total[part] for part in range(4)]
        totals.append(total)
    for part in range(4):
        out[pl.ds(part, share, stride=4), :] = lefts(totals[0][part], totals[1][part])
        out[pl.ds(share * 4 + part, share, stride=4), :] = rights(totals[0][part], totals[1][part])


def stack(strips, first):
    _, _, share, width = strips.shape

    def kernel(*refs):
        stack_kernel(first, *refs)

    return pl.pallas_call(
        kernel,
        in_specs=[pl.BlockSpec(memory_space=pltpu.VMEM)],
        out_shape=jax.ShapeDtypeStruct((share * 8, width), jnp.float32),
        name="stack",
    )(resident(strips))


def shards(fragments, layer_rank, pixel_count, slot_count, block_run, brick_order, interlace):
    _, _, owners, capacity, _, width = fragments.shape
    slots = interlace.shape[0]
    tiles = lax.axis_size("depth")
    bricks = lax.axis_size("brick")
    middle = tiles // 2
    first = [middle + 1, middle, *range(middle + 2, tiles), *range(middle - 2, middle), *range(middle - 2)]
    root = (lax.axis_size("tile") // 2 + 1) * bricks + bricks // 2
    runs = np.split(np.arange(owners, dtype=np.int32), 2)[::-1]
    runs[0][[0, root - owners // 2]] = runs[0][[root - owners // 2, 0]]
    order = np.concatenate(runs)
    blocks = blend(fragments[0, 0], layer_rank[0, 0], pixel_count[0, 0].T, root)
    groups = [
        [int(owners * (2 * chip + core) + owner) for run in runs for core in (1, 0) for owner in run]
        for chip in range(tiles // 2)
    ]
    sent = lax.all_to_all(
        blocks.reshape(2 * owners, 4, width),
        ("depth", "tile", "brick"),
        split_axis=0,
        concat_axis=0,
        tiled=True,
        axis_index_groups=groups,
    )
    own = jnp.concatenate([slot_count[0], brick_order, block_run[0, 0].T], axis=0)
    other = lax.ppermute(own, "depth", [(place, place ^ 1) for place in range(tiles)])
    in_front = lax.axis_index("depth") % 2 == 0
    index = jnp.stack([jnp.where(in_front, own, other), jnp.where(in_front, other, own)])
    plans = plan(index, interlace.reshape(1, slots), jnp.asarray(order).reshape(1, owners), capacity, tiles)
    strip = compose_strip(sent.reshape(owners * 8, width), *plans, tiles, first)
    strips = lax.all_to_all(
        strip,
        "depth",
        split_axis=0,
        concat_axis=0,
        tiled=True,
        axis_index_groups=[first],
    )
    return stack(strips, first).reshape(1, 1, slots // tiles, 4, width)


def solution(mesh):
    return jax.shard_map(
        shards,
        mesh=mesh,
        in_specs=(
            P("depth", ("tile", "brick"), None, None, None, None),
            P("depth", ("tile", "brick"), None, None, None),
            P("depth", ("tile", "brick"), None, None),
            P("depth", ("tile", "brick"), None),
            P("depth", ("tile", "brick"), None, None),
            P("depth", None),
            P(),
        ),
        out_specs=P(("tile", "brick"), "depth", None, None, None),
        check_vma=False,
    )
```
